32 devices in a mesh: req: 8 (over z, y), tp: 4 (over x, core).
Axes of the slice: x: 2, y: 2, z: 4, core: 2. Of those that a mesh axis runs over, the one named last changes fastest.
Arguments:
- tokens: bfloat16 [16384, 8192], P('req', 'tp'), may hold values from -6 to 6
- base_projection_weight: bfloat16 [8192, 2048], P('tp'), may hold values from -0.0625 to 0.0625
- adapter_down_maps: bfloat16 [128, 8192, 128], P('req', 'tp'), may hold values from -0.0625 to 0.0625
- adapter_up_maps: bfloat16 [128, 64, 2048], P('req', None, 'tp'), may hold values from -0.75 to 0.75
- block_adapter_ids: int32 [128], replicated, may hold values from 0 to 128, as said below
- adapter_storage_entry: int32 [128], replicated, may hold values from 0 to 127, as said below
Outputs:
- key_value: bfloat16 [16384, 2048], P('req', 'tp')
The draws below stay inside these ranges and needn't reach their ends.
Inputs may be any that keep to these rules, and one draw needn't show every extreme that they name: `block_adapter_ids`: ids are 0 (base model) or 1 to 128. Adapter k is held by req index adapter_storage_entry[k - 1] // 16. Among the 16 blocks of one req index (blocks i * 16 to i * 16 + 15) at most 2 name adapters held by any one req index; in every draw one req index receives exactly 2 blocks, all naming one adapter, from every req index. `adapter_storage_entry`: A permutation: each storage entry holds exactly one adapter.
All inputs are finite; a program needn't handle non-finite values.
Results may differ from the reference program's by a relative error of at most 0.014.
Values may be sent and summed in bfloat16 or wider, within the bound.
A program may use at most 128 MiB of HBM per device.

```python
import jax
import jax.numpy as jnp
from jax import lax

MODEL_WIDTH = 8192
KEY_WIDTH = 1024
ADAPTER_RANK = 64
BLOCK = 128
CAP = 2
BLK_DEV = 16
ADP_DEV = 16
ROWS = 16384
BLOCKS = 128
ADAPTER_TOTAL = 128
N_REQ = 8
N_TP = 4


def adapter_tables(key):
    folded = jax.random.fold_in(key, 31)
    key_slot, key_hot, key_local, key_perm, key_pick, key_other, key_kind, key_order = jax.random.split(folded, 8)
    slot_map = jax.random.permutation(key_slot, ADAPTER_TOTAL).astype(jnp.int32)
    inverse = jnp.zeros((ADAPTER_TOTAL,), jnp.int32).at[slot_map].set(jnp.arange(ADAPTER_TOTAL, dtype=jnp.int32))
    lane_count = BLK_DEV // CAP
    hot_owner = jax.random.randint(key_hot, (), 0, N_REQ).astype(jnp.int32)
    hot_local = jax.random.randint(key_local, (), 0, ADP_DEV).astype(jnp.int32)
    others = jax.vmap(lambda subkey: jax.random.permutation(subkey, N_REQ - 1))(jax.random.split(key_perm, N_REQ)).astype(jnp.int32)
    lane_owner = jnp.concatenate([jnp.full((N_REQ, 1), hot_owner, jnp.int32), (hot_owner + 1 + others[:, :lane_count - 1]) % N_REQ], axis=1)
    picked = jax.random.randint(key_pick, (N_REQ, lane_count), 0, ADP_DEV).astype(jnp.int32)
    lane_local = picked.at[:, 0].set(hot_local)
    first_ids = inverse[lane_owner * ADP_DEV + lane_local] + 1
    other_local = jax.random.randint(key_other, (N_REQ, lane_count), 0, ADP_DEV).astype(jnp.int32)
    other_ids = inverse[lane_owner * ADP_DEV + other_local] + 1
    second_kind = jax.random.randint(key_kind, (N_REQ, lane_count), 0, 4).astype(jnp.int32).at[:, 0].set(2)
    second = jnp.where(second_kind == 0, 0, jnp.where(second_kind == 1, other_ids, first_ids))
    paired = jnp.stack([first_ids, second], axis=2).reshape(N_REQ, lane_count * 2)
    block_order = jax.vmap(lambda subkey: jax.random.permutation(subkey, BLK_DEV))(jax.random.split(key_order, N_REQ)).astype(jnp.int32)
    blocks = jnp.take_along_axis(paired, block_order, axis=1)
    return (slot_map, blocks.reshape(N_REQ * BLK_DEV).astype(jnp.int32))


def draw_adapter_storage_entry(key, part):
    return adapter_tables(key)[0]


def draw_block_adapter_ids(key, part):
    return adapter_tables(key)[1]


def block_scale(stream_key, extent, cuts, smallest, largest):
    def one(axis_at, shards_of):
        heights = jax.random.uniform(jax.random.fold_in(jax.random.fold_in(stream_key, 6), axis_at), (shards_of,), jnp.float32, smallest / len(cuts), largest / len(cuts))
        return jnp.repeat(jnp.exp(heights), extent[axis_at] // shards_of).reshape((-1,) + (1,) * (len(extent) - axis_at - 1))

    gain = one(*cuts[0])
    for cut in cuts[1:]:
        gain = gain * one(*cut)
    return gain


def scatter_about(key, dims, deviation, limit, cuts=(), kind=jnp.bfloat16):
    values = jax.random.normal(key, dims, jnp.float32) * deviation
    if len(cuts) > 0:
        values = block_scale(key, dims, cuts, -0.22, 0.18) * values
    return jnp.clip(values, min=-limit, max=limit).astype(kind)


def setup_inputs(seed: int = 0) -> dict:
    key_list = jax.random.split(jax.random.key(seed), 7)
    return {
        "tokens": scatter_about(key_list[0], (ROWS, MODEL_WIDTH), 1.0, 6.0, ((0, 8), (1, 4))),
        "base_projection_weight": scatter_about(key_list[1], (MODEL_WIDTH, 2 * KEY_WIDTH), MODEL_WIDTH ** -0.5, 0.0625, ((0, 4),)),
        "adapter_down_maps": scatter_about(key_list[2], (ADAPTER_TOTAL, MODEL_WIDTH, 2 * ADAPTER_RANK), MODEL_WIDTH ** -0.5, 0.0625, ((0, 8), (1, 4))),
        "adapter_up_maps": scatter_about(key_list[3], (ADAPTER_TOTAL, ADAPTER_RANK, 2 * KEY_WIDTH), ADAPTER_RANK ** -0.5, 0.75, ((0, 8), (2, 4))),
        "block_adapter_ids": draw_block_adapter_ids(jax.random.fold_in(key_list[6], 71), 0),
        "adapter_storage_entry": draw_adapter_storage_entry(jax.random.fold_in(key_list[6], 71), 0),
    }


def reference(tokens, base_projection_weight, adapter_down_maps, adapter_up_maps, block_adapter_ids, adapter_storage_entry):
    group_width = MODEL_WIDTH // N_TP
    base_sum = jnp.zeros((tokens.shape[0], 2 * KEY_WIDTH), jnp.float32)
    for group_index in range(N_TP):
        offset = group_index * group_width
        product = jnp.dot(tokens[:, offset:offset + group_width], base_projection_weight[offset:offset + group_width], preferred_element_type=jnp.float32).astype(jnp.bfloat16)
        base_sum = base_sum + lax.optimization_barrier(product).astype(jnp.float32)
    entries = adapter_storage_entry[jnp.maximum(block_adapter_ids - 1, 0)].astype(jnp.int32)
    blocks = tokens.reshape(BLOCKS, BLOCK, MODEL_WIDTH)

    def one_block(inputs):
        block_rows, storage_index, adapter_id = inputs
        down_projected = jnp.dot(block_rows, adapter_down_maps[storage_index], preferred_element_type=jnp.float32).astype(jnp.bfloat16)
        up_weight_matrix = adapter_up_maps[storage_index]
        key_part = jnp.dot(down_projected[:, :ADAPTER_RANK], up_weight_matrix[:, :KEY_WIDTH], preferred_element_type=jnp.float32)
        value_part = jnp.dot(down_projected[:, ADAPTER_RANK:], up_weight_matrix[:, KEY_WIDTH:], preferred_element_type=jnp.float32)
        block_delta = jnp.concatenate([key_part, value_part], axis=1).astype(jnp.bfloat16)
        return jnp.where(adapter_id > 0, block_delta, jnp.zeros_like(block_delta))

    deltas = lax.map(one_block, (blocks, entries, block_adapter_ids))
    deltas = lax.optimization_barrier(deltas).reshape(BLOCKS * BLOCK, 2 * KEY_WIDTH).astype(jnp.float32)
    return (base_sum + deltas).astype(jnp.bfloat16)
```

```python
import functools

import jax
import jax.numpy as jnp
from jax import lax
from jax.experimental import pallas as pl
from jax.experimental.pallas import tpu as pltpu
from jax.sharding import PartitionSpec as P

BLOCK = 128
LANES = 128
MESH = pl.DeviceIdType.MESH
VMEM_BYTES = 62 * 1024 * 1024


def offsets(n_req, blocks):
    names = (
        ("direct", n_req), ("extra", n_req), ("far", n_req // 2), ("pick", n_req),
        ("blk0", n_req), ("blk1", n_req), ("differ", n_req),
        ("own", blocks), ("second", blocks), ("other", blocks), ("live", blocks),
    )
    place, at = {}, 0
    for name, count in names:
        place[name] = at
        at += count
    return place, at


def body(
    n_req, n_tp, slots, place,
    tbl, tok_in, w_in, down_in, up_in, out,
    own, tok, wgt, s_near, s_nearx, s_far, s_farx, relay, s_relay, direct, extra,
    cs, cr, xr, part, landed, total,
    load_sem, w_sem, near_ss, nearx_ss, far_ss, farx_ss, relay_ss, direct_rs, extra_rs, relay_rs,
    core_ss, core_rs, x_ss, x_rs, part_ss, part_rs, out_sem,
):
    half = n_req // 2
    chips = n_tp // 2
    me = lax.axis_index("req")
    tp = lax.axis_index("tp")
    base = (me // half) * half
    mirror = n_req - 1 - me
    blocks, _, feat = tok.shape
    cols = wgt.shape[2]
    rank = part.shape[3] // 2
    up_rows = own.shape[1] - feat
    chip, core = tp // 2, tp % 2
    mate = tp + 1 - 2 * core

    def near(k):
        return base + lax.rem(me - base + k, half)

    def far(k):
        return (half - base) + lax.rem(me - base + k, half)

    loads = [pltpu.make_async_copy(down_in, own.at[:, pl.ds(0, feat)], load_sem.at[0])]
    for c in range(cols // LANES):
        loads.append(
            pltpu.make_async_copy(
                up_in.at[:, :, pl.ds(c * LANES, LANES)],
                own.at[:, pl.ds(feat + c * rank, rank)],
                load_sem.at[1 + c],
            )
        )
    tok_load = pltpu.make_async_copy(tok_in, tok, load_sem.at[1 + cols // LANES])

    def target(step):
        where = lax.rem(chip + 1 + step % chips, chips)
        return 2 * where + (1 - core if step < chips else core)

    def w_load(step):
        at = pl.multiple_of(target(step) * cols, cols)
        return pltpu.make_async_copy(w_in.at[:, pl.ds(at, cols)], wgt.at[step], w_sem.at[step])

    for copy in loads:
        copy.start()
    tok_load.start()
    for step in range(n_tp):
        w_load(step).start()

    barrier = pltpu.get_barrier_semaphore()
    for d in range(1, n_req):
        pl.semaphore_signal(
            barrier, inc=1, device_id={"req": lax.rem(me + d, n_req)}, device_id_type=MESH
        )
    for d in range(1, n_tp):
        pl.semaphore_signal(
            barrier, inc=1, device_id={"tp": lax.rem(tp + d, n_tp)}, device_id_type=MESH
        )
    pl.semaphore_wait(barrier, n_req + n_tp - 2)

    def send(src, dst, ss, rs, to):
        return pltpu.make_async_remote_copy(
            src_ref=src, dst_ref=dst, send_sem=ss, recv_sem=rs,
            device_id={"req": to}, device_id_type=MESH,
        )

    def farx_copy(j):
        return send(s_farx.at[j], relay.at[j], farx_ss.at[j], relay_rs.at[j], mirror)

    def nearx_copy(k):
        return send(s_nearx.at[k - 1], extra.at[me], nearx_ss.at[k - 1], extra_rs.at[me], near(k))

    def near_copy(k):
        return send(s_near.at[k - 1], direct.at[me], near_ss.at[k - 1], direct_rs.at[me], near(k))

    def far_copy(k):
        return send(s_far.at[k], direct.at[me], far_ss.at[k], direct_rs.at[me], far(k))

    def relay_copy(k):
        return send(
            s_relay.at[k - 1], extra.at[mirror], relay_ss.at[k - 1], extra_rs.at[mirror], near(k)
        )

    def got(ref, rs, o):
        pltpu.make_async_remote_copy(
            src_ref=ref.at[o], dst_ref=ref.at[o], send_sem=core_ss.at[0], recv_sem=rs.at[o],
            device_id={"req": mirror}, device_id_type=MESH,
        ).wait_recv()

    for copy in loads:
        copy.wait()
    for j in range(slots):
        s_farx[j] = own[tbl[place["far"] + j]]
        farx_copy(j).start()

    @pl.loop(1, half)
    def _(k):
        s_near[k - 1] = own[tbl[place["direct"] + near(k)]]
        near_copy(k).start()
        s_nearx[k - 1] = own[tbl[place["extra"] + near(k)]]
        nearx_copy(k).start()

    @pl.loop(0, half)
    def _(k):
        s_far[k] = own[tbl[place["direct"] + far(k)]]

    direct[me] = own[tbl[place["direct"] + me]]
    extra[me] = own[tbl[place["extra"] + me]]

    tok_load.wait()
    tile = 4 if blocks % 4 == 0 else 1

    def product(step, g):
        rows = tok[pl.ds(g * tile, tile)].reshape(tile * BLOCK, feat)
        return jnp.dot(rows, wgt[step], preferred_element_type=jnp.float32)

    def core_copy(q):
        return pltpu.make_async_remote_copy(
            src_ref=cs.at[q], dst_ref=cr.at[q], send_sem=core_ss.at[q], recv_sem=core_rs.at[q],
            device_id={"tp": mate}, device_id_type=MESH,
        )

    def x_copy(q):
        to = 2 * lax.rem(chip + 1 + q, chips) + core
        return pltpu.make_async_remote_copy(
            src_ref=cr.at[q], dst_ref=xr.at[q], send_sem=x_ss.at[q], recv_sem=x_rs.at[q],
            device_id={"tp": to}, device_id_type=MESH,
        )

    for q in range(chips):
        w_load(q).wait()

        @pl.loop(0, blocks // tile)
        def _(g):
            cs[q, pl.ds(g * tile, tile)] = product(q, g).astype(cs.dtype).reshape(tile, BLOCK, cols)

        core_copy(q).start()
    for q in range(chips):
        w_load(chips + q).wait()
        core_copy(q).wait()

        @pl.loop(0, blocks // tile)
        def _(g):
            at = pl.ds(g * tile, tile)
            mine = product(chips + q, g).reshape(tile, BLOCK, cols)
            cr[q, at] = (mine + cr[q, at].astype(jnp.float32)).astype(cr.dtype)

        if q < chips - 1:
            x_copy(q).start()

    for j in range(slots):
        farx_copy(j).wait_send()

    @pl.loop(0, half)
    def _(k):
        far_copy(k).start()

    for j in range(slots):
        farx_copy(j).wait_recv()
    extra[mirror] = relay[tbl[place["pick"] + me]]

    @pl.loop(1, half)
    def _(k):
        s_relay[k - 1] = relay[tbl[place["pick"] + near(k)]]
        relay_copy(k).start()

    def part_copy(d, o):
        to = lax.rem(tp + d, n_tp)
        return pltpu.make_async_remote_copy(
            src_ref=part.at[to // chips, o], dst_ref=landed.at[d - 1, o],
            send_sem=part_ss.at[d - 1, o], recv_sem=part_rs.at[d - 1, o],
            device_id={"tp": to}, device_id_type=MESH,
        )

    def shrink(o):
        first = tok[tbl[place["blk0"] + o]]
        later = tok[tbl[place["blk1"] + o]]
        differ = tbl[place["differ"] + o] > 0
        one = jnp.dot(first, direct[o, :feat], preferred_element_type=jnp.float32)
        two = jnp.dot(later, direct[o, :feat], preferred_element_type=jnp.float32)
        alt = jnp.dot(later, extra[o, :feat], preferred_element_type=jnp.float32)
        two = jnp.where(differ, alt, two).astype(part.dtype)
        one = one.astype(part.dtype)
        part[0, o] = jnp.concatenate([one[:, :rank], two[:, :rank]], axis=1)
        part[1, o] = jnp.concatenate([one[:, rank:], two[:, rank:]], axis=1)
        for d in range(1, n_tp):
            part_copy(d, o).start()

    shrink(me)

    @pl.loop(1, half)
    def _(k):
        o = near(k)
        got(direct, direct_rs, o)
        got(extra, extra_rs, o)
        shrink(o)

    @pl.loop(0, half)
    def _(k):
        o = far(k)

        @pl.when(o != mirror)
        def _():
            got(extra, extra_rs, o)

        got(direct, direct_rs, o)
        shrink(o)

    for q in range(chips - 1):
        x_copy(q).wait()

    @pl.loop(0, n_req)
    def _(o):
        acc = part[tp // chips, o].astype(jnp.float32)
        for d in range(1, n_tp):
            part_copy(d, o).wait()
            acc = acc + landed[d - 1, o].astype(jnp.float32)
        total[o] = acc.astype(total.dtype)

    @pl.loop(0, blocks)
    def _(b):
        o = tbl[place["own"] + b]
        both = total[o]
        mine = jnp.where(tbl[place["second"] + b] > 0, both[:, rank:], both[:, :rank])
        up = jnp.where(
            tbl[place["other"] + b] > 0,
            extra[o, pl.ds(feat, up_rows)],
            direct[o, pl.ds(feat, up_rows)],
        )
        live = tbl[place["live"] + b] > 0
        for c in range(cols // LANES):
            lanes = slice(c * LANES, (c + 1) * LANES)
            delta = jnp.dot(
                mine, up[c * rank:(c + 1) * rank], preferred_element_type=jnp.float32
            )
            delta = delta.astype(jnp.bfloat16).astype(jnp.float32)
            acc = cr[chips - 1, b, :, lanes].astype(jnp.float32)
            for q in range(chips - 1):
                acc = acc + xr[q, b, :, lanes].astype(jnp.float32)
            cr[chips - 1, b, :, lanes] = (acc + jnp.where(live, delta, 0.0)).astype(cr.dtype)

    store = pltpu.make_async_copy(cr.at[chips - 1], out, out_sem)
    store.start()

    @pl.loop(1, half)
    def _(k):
        near_copy(k).wait_send()
        nearx_copy(k).wait_send()
        relay_copy(k).wait_send()

    @pl.loop(0, half)
    def _(k):
        far_copy(k).wait_send()

    store.wait()


def fused(tbl, tokens, weight, downs, ups, n_req, n_tp, slots, place):
    rows, feat = tokens.shape
    blocks = rows // BLOCK
    entries, _, width = downs.shape
    rank, cols = ups.shape[1:]
    slot_rows = feat + rank * cols // LANES
    half, chips = n_req // 2, n_tp // 2
    kind = tokens.dtype
    slot = (slot_rows, width)
    tiles = (blocks, BLOCK, cols)
    vmem = lambda *shape: pltpu.VMEM(shape, kind)
    dma = lambda *shape: pltpu.SemaphoreType.DMA(shape)
    any_spec = pl.BlockSpec(memory_space=pl.ANY)
    out = pl.pallas_call(
        functools.partial(body, n_req, n_tp, slots, place),
        in_specs=[pl.BlockSpec(memory_space=pltpu.SMEM)] + [any_spec] * 4,
        out_specs=any_spec,
        out_shape=jax.ShapeDtypeStruct(tiles, kind),
        scratch_shapes=[
            vmem(entries, *slot),
            vmem(blocks, BLOCK, feat),
            vmem(n_tp, feat, cols),
            vmem(half - 1, *slot),
            vmem(half - 1, *slot),
            vmem(half, *slot),
            vmem(slots, *slot),
            vmem(slots, *slot),
            vmem(half - 1, *slot),
            vmem(n_req, *slot),
            vmem(n_req, *slot),
            vmem(chips, *tiles),
            vmem(chips, *tiles),
            vmem(chips - 1, *tiles),
            vmem(2, n_req, BLOCK, width),
            vmem(n_tp - 1, n_req, BLOCK, width),
            vmem(n_req, BLOCK, width),
            dma(2 + cols // LANES),
            dma(n_tp),
            dma(half - 1),
            dma(half - 1),
            dma(half),
            dma(slots),
            dma(half - 1),
            dma(n_req),
            dma(n_req),
            dma(slots),
            dma(chips),
            dma(chips),
            dma(chips - 1),
            dma(chips - 1),
            dma(n_tp - 1, n_req),
            dma(n_tp - 1, n_req),
            pltpu.SemaphoreType.DMA,
        ],
        compiler_params=pltpu.CompilerParams(
            collective_id=slots, has_side_effects=True, vmem_limit_bytes=VMEM_BYTES
        ),
        cost_estimate=pl.CostEstimate(
            flops=2 * rows * feat * (n_tp * cols + width),
            bytes_accessed=4 * rows * feat,
            transcendentals=0,
        ),
    )(tbl, tokens.reshape(blocks, BLOCK, feat), weight, downs, ups)
    return out.reshape(rows, cols)


def routes(ids, storage, me, n_req, entries):
    half = n_req // 2
    ids_all = ids.reshape(n_req, -1)
    blocks = ids_all.shape[1]
    place, _ = offsets(n_req, blocks)
    stored = storage[jnp.maximum(ids_all - 1, 0)]
    owner = jnp.where(ids_all > 0, stored // entries, -1)
    local = stored % entries
    pos = jnp.arange(blocks, dtype=jnp.int32)
    same = (owner[:, :, None] == owner[:, None, :]) & (pos[None, :] < pos[:, None])[None]
    nth = jnp.sum(same, axis=2, dtype=jnp.int32)
    reqs = jnp.arange(n_req, dtype=jnp.int32)
    hit = owner[:, None, :] == reqs[None, :, None]
    hit0 = hit & (nth == 0)[:, None]
    hit1 = hit & (nth == 1)[:, None]
    take = lambda mask, what: jnp.sum(jnp.where(mask, what, 0), axis=2, dtype=jnp.int32)
    loc0, loc1 = take(hit0, local[:, None]), take(hit1, local[:, None])
    blk0, blk1 = take(hit0, pos[None, None]), take(hit1, pos[None, None])
    differ = jnp.any(hit1, axis=2) & (loc0 != loc1)
    far = differ & ((reqs // half)[:, None] != (reqs // half)[None, :])
    before = reqs[None, :] < reqs[:, None]
    nth_far = jnp.sum(far[None] & before[:, :, None], axis=1, dtype=jnp.int32)
    need = jnp.max(jnp.sum(far, axis=0, dtype=jnp.int32))
    row = lambda a: lax.dynamic_index_in_dim(a, me, 0, keepdims=False)
    col = lambda a, at: lax.dynamic_index_in_dim(a, at, 1, keepdims=False)
    far_me, nth_me, loc1_me = col(far, me), col(nth_far, me), col(loc1, me)
    mirror = n_req - 1 - me
    slot = jnp.arange(half, dtype=jnp.int32)
    far_list = jnp.sum(
        jnp.where(far_me[None] & (nth_me[None] == slot[:, None]), loc1_me[None], 0),
        axis=1, dtype=jnp.int32,
    )
    pick = jnp.where(col(far, mirror), col(nth_far, mirror), 0)
    own_me, nth_b, differ_me = row(owner), row(nth), row(differ).astype(jnp.int32)
    other = jnp.sum(
        jnp.where((own_me[:, None] == reqs[None]) & (nth_b[:, None] == 1), differ_me[None], 0),
        axis=1, dtype=jnp.int32,
    )
    table = jnp.concatenate([
        col(loc0, me), loc1_me, far_list, pick, row(blk0), row(blk1), differ_me,
        jnp.maximum(own_me, 0), nth_b * (own_me >= 0), other, (own_me >= 0).astype(jnp.int32),
    ])
    return table.astype(jnp.int32), need, place


def per_device(tokens, weight, downs, ups, ids, storage):
    n_req, n_tp = lax.axis_size("req"), lax.axis_size("tp")
    me = lax.axis_index("req")
    table, need, place = routes(ids, storage, me, n_req, downs.shape[0])
    return fused(table, tokens, weight, downs, ups, n_req, n_tp, n_req // 2, place)


def solution(mesh):
    placed = (P("req", "tp"), P("tp", None), P("req", "tp", None), P("req", None, "tp"), P(), P())
    return jax.shard_map(
        per_device, mesh=mesh, in_specs=placed, out_specs=P("req", "tp"), check_vma=False
    )
```

```python
import functools

import jax
import jax.numpy as jnp
from jax import lax
from jax.experimental import pallas as pl
from jax.experimental.pallas import tpu as pltpu
from jax.sharding import PartitionSpec as P

BLOCK = 128
LANES = 128
MESH = pl.DeviceIdType.MESH
VMEM_BYTES = 62 * 1024 * 1024


PLANES = 4


def mirror_of(r, n_req):
    wide = n_req // PLANES
    return (PLANES - 1 - r // wide) * wide + r % wide


def offsets(n_req, blocks):
    names = (
        ("direct", n_req), ("extra", n_req), ("far", n_req // 2), ("pick", n_req),
        ("blk0", n_req), ("blk1", n_req), ("differ", n_req),
        ("own", blocks), ("second", blocks), ("other", blocks), ("live", blocks),
    )
    place, at = {}, 0
    for name, count in names:
        place[name] = at
        at += count
    return place, at


def body(
    n_req, n_tp, slots, place,
    tbl, tok_in, w_in, down_in, up_in, out,
    own, tok, wgt, s_near, s_nearx, s_far, s_farx, relay, s_relay, direct, extra,
    cs, cr, xr, part, landed, total,
    load_sem, w_sem, near_ss, nearx_ss, far_ss, farx_ss, relay_ss, direct_rs, extra_rs, relay_rs,
    core_ss, core_rs, x_ss, x_rs, part_ss, part_rs, out_sem,
):
    half = n_req // 2
    chips = n_tp // 2
    me = lax.axis_index("req")
    tp = lax.axis_index("tp")
    base = (me // half) * half
    mirror = mirror_of(me, n_req)
    inner = (me >= n_req // 4) & (me < n_req - n_req // 4)
    few = jnp.where(inner, slots[0], slots[1])
    blocks, _, feat = tok.shape
    cols = wgt.shape[2]
    rank = part.shape[3] // 2
    up_rows = own.shape[1] - feat
    chip, core = tp // 2, tp % 2
    mate = tp + 1 - 2 * core

    def near(k):
        return base + lax.rem(me - base + k, half)

    def far(k):
        return (half - base) + lax.rem(me - base + k, half)

    loads = [pltpu.make_async_copy(down_in, own.at[:, pl.ds(0, feat)], load_sem.at[0])]
    for c in range(cols // LANES):
        loads.append(
            pltpu.make_async_copy(
                up_in.at[:, :, pl.ds(c * LANES, LANES)],
                own.at[:, pl.ds(feat + c * rank, rank)],
                load_sem.at[1 + c],
            )
        )
    tok_load = pltpu.make_async_copy(tok_in, tok, load_sem.at[1 + cols // LANES])

    def target(step):
        where = lax.rem(chip + 1 + step % chips, chips)
        return 2 * where + (1 - core if step < chips else core)

    def w_load(step):
        at = pl.multiple_of(target(step) * cols, cols)
        return pltpu.make_async_copy(w_in.at[:, pl.ds(at, cols)], wgt.at[step], w_sem.at[step])

    for copy in loads:
        copy.start()
    tok_load.start()
    for step in range(n_tp):
        w_load(step).start()

    barrier = pltpu.get_barrier_semaphore()
    for d in range(1, n_req):
        pl.semaphore_signal(
            barrier, inc=1, device_id={"req": lax.rem(me + d, n_req)}, device_id_type=MESH
        )
    for d in range(1, n_tp):
        pl.semaphore_signal(
            barrier, inc=1, device_id={"tp": lax.rem(tp + d, n_tp)}, device_id_type=MESH
        )
    pl.semaphore_wait(barrier, n_req + n_tp - 2)

    def send(src, dst, ss, rs, to):
        return pltpu.make_async_remote_copy(
            src_ref=src, dst_ref=dst, send_sem=ss, recv_sem=rs,
            device_id={"req": to}, device_id_type=MESH,
        )

    def farx_copy(j):
        return send(s_farx.at[j], relay.at[j], farx_ss.at[j], relay_rs.at[j], mirror)

    def nearx_copy(k):
        return send(s_nearx.at[k - 1], extra.at[me], nearx_ss.at[k - 1], extra_rs.at[me], near(k))

    def near_copy(k):
        return send(s_near.at[k - 1], direct.at[me], near_ss.at[k - 1], direct_rs.at[me], near(k))

    def far_copy(k):
        return send(s_far.at[k], direct.at[me], far_ss.at[k], direct_rs.at[me], far(k))

    def relay_copy(k):
        return send(
            s_relay.at[k - 1], extra.at[mirror], relay_ss.at[k - 1], extra_rs.at[mirror], near(k)
        )

    def got(ref, rs, o):
        pltpu.make_async_remote_copy(
            src_ref=ref.at[o], dst_ref=ref.at[o], send_sem=core_ss.at[0], recv_sem=rs.at[o],
            device_id={"req": mirror}, device_id_type=MESH,
        ).wait_recv()

    for copy in loads:
        copy.wait()

    @pl.loop(0, few)
    def _(j):
        s_farx[j] = own[tbl[place["far"] + j]]
        farx_copy(j).start()

    @pl.loop(1, half)
    def _(k):
        s_near[k - 1] = own[tbl[place["direct"] + near(k)]]
        near_copy(k).start()
        s_nearx[k - 1] = own[tbl[place["extra"] + near(k)]]
        nearx_copy(k).start()

    @pl.loop(0, half)
    def _(k):
        s_far[k] = own[tbl[place["direct"] + far(k)]]
        far_copy(k).start()

    direct[me] = own[tbl[place["direct"] + me]]
    extra[me] = own[tbl[place["extra"] + me]]

    tok_load.wait()
    tile = 4 if blocks % 4 == 0 else 1

    def product(step, g):
        rows = tok[pl.ds(g * tile, tile)].reshape(tile * BLOCK, feat)
        return jnp.dot(rows, wgt[step], preferred_element_type=jnp.float32)

    def core_copy(q):
        return pltpu.make_async_remote_copy(
            src_ref=cs.at[q], dst_ref=cr.at[q], send_sem=core_ss.at[q], recv_sem=core_rs.at[q],
            device_id={"tp": mate}, device_id_type=MESH,
        )

    def x_copy(q):
        to = 2 * lax.rem(chip + 1 + q, chips) + core
        return pltpu.make_async_remote_copy(
            src_ref=cr.at[q], dst_ref=xr.at[q], send_sem=x_ss.at[q], recv_sem=x_rs.at[q],
            device_id={"tp": to}, device_id_type=MESH,
        )

    for q in range(chips):
        w_load(q).wait()

        @pl.loop(0, blocks // tile)
        def _(g):
            cs[q, pl.ds(g * tile, tile)] = product(q, g).astype(cs.dtype).reshape(tile, BLOCK, cols)

        core_copy(q).start()
    for q in range(chips):
        w_load(chips + q).wait()
        core_copy(q).wait()

        @pl.loop(0, blocks // tile)
        def _(g):
            at = pl.ds(g * tile, tile)
            mine = product(chips + q, g).reshape(tile, BLOCK, cols)
            cr[q, at] = (mine + cr[q, at].astype(jnp.float32)).astype(cr.dtype)

        if q < chips - 1:
            x_copy(q).start()

    @pl.loop(0, few)
    def _(j):
        farx_copy(j).wait()

    extra[mirror] = relay[tbl[place["pick"] + me]]

    @pl.loop(1, half)
    def _(k):
        s_relay[k - 1] = relay[tbl[place["pick"] + near(k)]]
        relay_copy(k).start()

    def part_copy(d, o):
        to = lax.rem(tp + d, n_tp)
        return pltpu.make_async_remote_copy(
            src_ref=part.at[to // chips, o], dst_ref=landed.at[d - 1, o],
            send_sem=part_ss.at[d - 1, o], recv_sem=part_rs.at[d - 1, o],
            device_id={"tp": to}, device_id_type=MESH,
        )

    def shrink(o):
        first = tok[tbl[place["blk0"] + o]]
        later = tok[tbl[place["blk1"] + o]]
        differ = tbl[place["differ"] + o] > 0
        one = jnp.dot(first, direct[o, :feat], preferred_element_type=jnp.float32)
        two = jnp.dot(later, direct[o, :feat], preferred_element_type=jnp.float32)
        alt = jnp.dot(later, extra[o, :feat], preferred_element_type=jnp.float32)
        two = jnp.where(differ, alt, two).astype(part.dtype)
        one = one.astype(part.dtype)
        part[0, o] = jnp.concatenate([one[:, :rank], two[:, :rank]], axis=1)
        part[1, o] = jnp.concatenate([one[:, rank:], two[:, rank:]], axis=1)
        for d in range(1, n_tp):
            part_copy(d, o).start()

    shrink(me)

    @pl.loop(1, half)
    def _(k):
        o = near(k)
        got(direct, direct_rs, o)
        got(extra, extra_rs, o)
        shrink(o)

    @pl.loop(0, half)
    def _(k):
        o = far(k)

        @pl.when(o != mirror)
        def _():
            got(extra, extra_rs, o)

        got(direct, direct_rs, o)
        shrink(o)

    for q in range(chips - 1):
        x_copy(q).wait()

    @pl.loop(0, n_req)
    def _(o):
        acc = part[tp // chips, o].astype(jnp.float32)
        for d in range(1, n_tp):
            part_copy(d, o).wait()
            acc = acc + landed[d - 1, o].astype(jnp.float32)
        total[o] = acc.astype(total.dtype)

    @pl.loop(0, blocks)
    def _(b):
        o = tbl[place["own"] + b]
        both = total[o]
        mine = jnp.where(tbl[place["second"] + b] > 0, both[:, rank:], both[:, :rank])
        up = jnp.where(
            tbl[place["other"] + b] > 0,
            extra[o, pl.ds(feat, up_rows)],
            direct[o, pl.ds(feat, up_rows)],
        )
        live = tbl[place["live"] + b] > 0
        for c in range(cols // LANES):
            lanes = slice(c * LANES, (c + 1) * LANES)
            delta = jnp.dot(
                mine, up[c * rank:(c + 1) * rank], preferred_element_type=jnp.float32
            )
            delta = delta.astype(jnp.bfloat16).astype(jnp.float32)
            acc = cr[chips - 1, b, :, lanes].astype(jnp.float32)
            for q in range(chips - 1):
                acc = acc + xr[q, b, :, lanes].astype(jnp.float32)
            cr[chips - 1, b, :, lanes] = (acc + jnp.where(live, delta, 0.0)).astype(cr.dtype)

    store = pltpu.make_async_copy(cr.at[chips - 1], out, out_sem)
    store.start()

    @pl.loop(1, half)
    def _(k):
        near_copy(k).wait_send()
        nearx_copy(k).wait_send()
        relay_copy(k).wait_send()

    @pl.loop(0, half)
    def _(k):
        far_copy(k).wait_send()

    store.wait()


def fused(tbl, tokens, weight, downs, ups, n_req, n_tp, slots, place, ident):
    rows, feat = tokens.shape
    blocks = rows // BLOCK
    entries, _, width = downs.shape
    rank, cols = ups.shape[1:]
    slot_rows = feat + rank * cols // LANES
    half, chips = n_req // 2, n_tp // 2
    kind = tokens.dtype
    slot = (slot_rows, width)
    tiles = (blocks, BLOCK, cols)
    vmem = lambda *shape: pltpu.VMEM(shape, kind)
    dma = lambda *shape: pltpu.SemaphoreType.DMA(shape)
    any_spec = pl.BlockSpec(memory_space=pl.ANY)
    out = pl.pallas_call(
        functools.partial(body, n_req, n_tp, slots, place),
        in_specs=[pl.BlockSpec(memory_space=pltpu.SMEM)] + [any_spec] * 4,
        out_specs=any_spec,
        out_shape=jax.ShapeDtypeStruct(tiles, kind),
        scratch_shapes=[
            vmem(entries, *slot),
            vmem(blocks, BLOCK, feat),
            vmem(n_tp, feat, cols),
            vmem(half - 1, *slot),
            vmem(half - 1, *slot),
            vmem(half, *slot),
            vmem(max(slots), *slot),
            vmem(max(slots), *slot),
            vmem(half - 1, *slot),
            vmem(n_req, *slot),
            vmem(n_req, *slot),
            vmem(chips, *tiles),
            vmem(chips, *tiles),
            vmem(chips - 1, *tiles),
            vmem(2, n_req, BLOCK, width),
            vmem(n_tp - 1, n_req, BLOCK, width),
            vmem(n_req, BLOCK, width),
            dma(2 + cols // LANES),
            dma(n_tp),
            dma(half - 1),
            dma(half - 1),
            dma(half),
            dma(max(slots)),
            dma(half - 1),
            dma(n_req),
            dma(n_req),
            dma(max(slots)),
            dma(chips),
            dma(chips),
            dma(chips - 1),
            dma(chips - 1),
            dma(n_tp - 1, n_req),
            dma(n_tp - 1, n_req),
            pltpu.SemaphoreType.DMA,
        ],
        compiler_params=pltpu.CompilerParams(
            collective_id=ident, has_side_effects=True, vmem_limit_bytes=VMEM_BYTES
        ),
        cost_estimate=pl.CostEstimate(
            flops=2 * rows * feat * (n_tp * cols + width),
            bytes_accessed=4 * rows * feat,
            transcendentals=0,
        ),
    )(tbl, tokens.reshape(blocks, BLOCK, feat), weight, downs, ups)
    return out.reshape(rows, cols)


def routes(ids, storage, me, n_req, entries):
    half = n_req // 2
    ids_all = ids.reshape(n_req, -1)
    blocks = ids_all.shape[1]
    place, _ = offsets(n_req, blocks)
    stored = storage[jnp.maximum(ids_all - 1, 0)]
    owner = jnp.where(ids_all > 0, stored // entries, -1)
    local = stored % entries
    pos = jnp.arange(blocks, dtype=jnp.int32)
    same = (owner[:, :, None] == owner[:, None, :]) & (pos[None, :] < pos[:, None])[None]
    nth = jnp.sum(same, axis=2, dtype=jnp.int32)
    reqs = jnp.arange(n_req, dtype=jnp.int32)
    hit = owner[:, None, :] == reqs[None, :, None]
    hit0 = hit & (nth == 0)[:, None]
    hit1 = hit & (nth == 1)[:, None]
    take = lambda mask, what: jnp.sum(jnp.where(mask, what, 0), axis=2, dtype=jnp.int32)
    loc0, loc1 = take(hit0, local[:, None]), take(hit1, local[:, None])
    blk0, blk1 = take(hit0, pos[None, None]), take(hit1, pos[None, None])
    differ = jnp.any(hit1, axis=2) & (loc0 != loc1)
    far = differ & ((reqs // half)[:, None] != (reqs // half)[None, :])
    kinds = jnp.arange(entries, dtype=jnp.int32)
    is0, is1 = loc0[:, :, None] == kinds, loc1[:, :, None] == kinds
    named = jnp.sum(far[:, :, None] & (is0 | is1), axis=0, dtype=jnp.int32)
    count = lambda which: jnp.sum(jnp.where(which, named[None], 0), axis=2, dtype=jnp.int32)
    lead = count(is0) * entries - loc0 > count(is1) * entries - loc1
    swap = far & lead
    loc0, loc1 = jnp.where(swap, loc1, loc0), jnp.where(swap, loc0, loc1)
    blk0, blk1 = jnp.where(swap, blk1, blk0), jnp.where(swap, blk0, blk1)
    chosen = far[:, :, None] & (loc1[:, :, None] == kinds)
    listed = jnp.any(chosen, axis=0)
    lower = kinds[None, :] < kinds[:, None]
    place_of = jnp.sum(listed[:, None, :] & lower[None], axis=2, dtype=jnp.int32)
    nth_far = jnp.sum(jnp.where(chosen, place_of[None], 0), axis=2, dtype=jnp.int32)
    amount = jnp.sum(listed, axis=1, dtype=jnp.int32)
    inner = (reqs >= n_req // 4) & (reqs < n_req - n_req // 4)
    need = (jnp.max(jnp.where(inner, amount, 0)), jnp.max(jnp.where(inner, 0, amount)))
    row = lambda a: lax.dynamic_index_in_dim(a, me, 0, keepdims=False)
    col = lambda a, at: lax.dynamic_index_in_dim(a, at, 1, keepdims=False)
    mirror = mirror_of(me, n_req)
    slot = jnp.arange(half, dtype=jnp.int32)
    far_list = jnp.sum(
        jnp.where(row(listed)[None] & (row(place_of)[None] == slot[:, None]), kinds[None], 0),
        axis=1, dtype=jnp.int32,
    )
    pick = col(nth_far, mirror)
    own_me, differ_me = row(owner), row(differ)
    mine = own_me[:, None] == reqs[None]
    turned = jnp.any(mine & row(swap)[None], axis=1)
    nth_b = jnp.where(turned, 1 - row(nth), row(nth))
    other = jnp.any(mine & differ_me[None], axis=1) & (nth_b == 1)
    table = jnp.concatenate([
        col(loc0, me), col(loc1, me), far_list, pick, row(blk0), row(blk1),
        differ_me.astype(jnp.int32), jnp.maximum(own_me, 0), jnp.where(own_me >= 0, nth_b, 0),
        other.astype(jnp.int32), (own_me >= 0).astype(jnp.int32),
    ])
    return table, need, place


def per_device(tokens, weight, downs, ups, ids, storage):
    n_req, n_tp = lax.axis_size("req"), lax.axis_size("tp")
    me = lax.axis_index("req")
    table, need, place = routes(ids, storage, me, n_req, downs.shape[0])
    half = n_req // 2
    plans = [(1, 1), (2, 1), (1, 2), (2, 2), (3, 3), (half, half)]
    enough = jnp.stack([(need[0] <= a) & (need[1] <= b) for a, b in plans])
    runs = [
        functools.partial(fused, n_req=n_req, n_tp=n_tp, slots=plan, place=place, ident=ident)
        for ident, plan in enumerate(plans)
    ]
    return lax.switch(jnp.argmax(enough), runs, table, tokens, weight, downs, ups)


def solution(mesh):
    placed = (P("req", "tp"), P("tp", None), P("req", "tp", None), P("req", None, "tp"), P(), P())
    return jax.shard_map(
        per_device, mesh=mesh, in_specs=placed, out_specs=P("req", "tp"), check_vma=False
    )
```

```python
import functools
import types

import jax
import jax.numpy as jnp
from jax import lax
from jax.experimental import pallas as pl
from jax.experimental.pallas import tpu as pltpu
from jax.sharding import PartitionSpec as P

BLOCK = 128
LANES = 128
MESH = pl.DeviceIdType.MESH
MOST = 4
PLANS = [(1, 1, 2), (2, 1, 3), (2, 2, 3), (3, 3, 3)]
EARLY = 2
VMEM_BYTES = 62 * 1024 * 1024


PLANES = 4


def mirror_of(r, n_req):
    wide = n_req // PLANES
    return (PLANES - 1 - r // wide) * wide + r % wide


def offsets(n_req, blocks):
    names = (
        ("direct", n_req), ("extra", n_req), ("far", n_req // 2), ("pick", n_req),
        ("blk0", n_req), ("blk1", n_req), ("differ", n_req),
        ("own", blocks), ("second", blocks), ("live", blocks),
        ("pool", MOST), ("pool_relay", MOST), ("pool_own", MOST), ("at", n_req),
    )
    place, at = {}, 0
    for name, count in names:
        place[name] = at
        at += count
    return place, at


def spots(slots, pool):
    own, near, passed = 0, 1, 2
    pools = passed + slots
    forward = pools + pool
    relayed = forward + pool
    return own, near, passed, pools, forward, relayed, relayed + slots


def route_body(n_req, blocks, entries, plans, place, ids, storage, table, plan, count, loc, blk, differ, rank, listed, amount, zneed):
    half, square = n_req // 2, n_req * n_req
    me = lax.axis_index("req")
    mirror = mirror_of(me, n_req)
    flag = lambda c: jnp.where(c, 1, 0).astype(jnp.int32)

    def put(name, k, value):
        table[place[name] + k] = value

    @pl.loop(0, square)
    def _(k):
        count[k] = 0
        loc[k] = 0
        loc[square + k] = 0
        blk[k] = 0
        blk[square + k] = 0
        rank[k] = 0

    def entry_of(k):
        ident = ids[k]
        entry = storage[jnp.maximum(ident - 1, 0)]
        return ident > 0, lax.div(entry, entries), lax.rem(entry, entries)

    @pl.loop(0, n_req)
    def _(i):
        for b in range(blocks):
            live, o, l = entry_of(i * blocks + b)
            at = i * n_req + o
            nth = count[at]
            count[at] = nth + flag(live)
            spot = jnp.where(live, nth * square + at, 2 * square)
            loc[spot] = l
            blk[spot] = b

    @pl.loop(0, n_req)
    def _(o):
        base = lax.div(o, half) * half
        ats = [(half - base + e) * n_req + o for e in range(half)]
        for e in range(half):
            at = (base + e) * n_req + o
            differ[at] = flag((count[at] == 2) & (loc[at] != loc[square + at]))
        a0 = [loc[at] for at in ats]
        a1 = [loc[square + at] for at in ats]
        two = [(count[at] == 2) & (x != y) for at, x, y in zip(ats, a0, a1)]
        names = lambda e, a: flag(two[e] & ((a0[e] == a) | (a1[e] == a)))
        used = jnp.int32(0)
        chosen, ranks = [], []
        for e, at in enumerate(ats):
            score0 = sum(names(f, a0[e]) for f in range(half)) * entries - a0[e]
            score1 = sum(names(f, a1[e]) for f in range(half)) * entries - a1[e]
            swap = two[e] & (score0 > score1)
            x = jnp.where(swap, a0[e], a1[e])
            loc[at] = jnp.where(swap, a1[e], a0[e])
            loc[square + at] = x
            b0, b1 = blk[at], blk[square + at]
            blk[at] = jnp.where(swap, b1, b0)
            blk[square + at] = jnp.where(swap, b0, b1)
            differ[at] = flag(two[e])
            mine, new = used, two[e]
            for f in range(e):
                same = two[e] & two[f] & (chosen[f] == x)
                mine = jnp.where(same, ranks[f], mine)
                new = new & jnp.logical_not(same)
            rank[at] = jnp.where(two[e], mine, 0)
            listed[jnp.where(new, o * half + mine, n_req * half)] = x
            used = used + flag(new)
            chosen.append(x)
            ranks.append(mine)
        amount[o] = used

    @pl.loop(0, n_req)
    def _(k):
        put("direct", k, loc[k * n_req + me])
        put("extra", k, loc[square + k * n_req + me])
        put("pick", k, rank[k * n_req + mirror])
        put("blk0", k, blk[me * n_req + k])
        put("blk1", k, blk[square + me * n_req + k])
        put("differ", k, differ[me * n_req + k])

    for k in range(half):
        put("far", k, jnp.where(k < amount[me], listed[me * half + k], 0))

    for b in range(blocks):
        live, o, _ = entry_of(me * blocks + b)
        at = me * n_req + o
        second = flag(live & (blk[at] != b))
        put("own", b, o)
        put("second", b, second)
        put("live", b, flag(live))

    plan[0] = len(plans)
    if not plans:
        return
    mate = lambda r: r + 1 - 2 * lax.rem(r, 2)
    zmate = lambda r: r + 2 - 4 * lax.rem(lax.div(r, 2), 2)
    need = []
    for p in range(PLANES):
        x, y = amount[2 * p], amount[2 * p + 1]
        need.append(jnp.maximum(jnp.maximum(x, y), 1))
    inside, outside = jnp.maximum(need[1], need[2]), jnp.maximum(need[0], need[3])

    deep = max(max(c_in, c_out) for c_in, c_out, _ in plans)
    for k in range(deep * n_req + 1):
        zneed[k] = 0

    def relayed(i, o):
        return mirror_of(o, n_req), rank[i * n_req + o]

    @pl.loop(0, n_req)
    def _(o):
        base = lax.div(o, half) * half
        for e in range(half):
            i = half - base + e
            chip, slot = relayed(i, o)
            want = (differ[i * n_req + o] > 0) & (lax.div(i, 2) != lax.div(chip, 2))
            zneed[jnp.where(want & (slot < deep), deep * chip + slot, deep * n_req)] = 1

    def pool_of(m):
        a = differ[zmate(m) * n_req + m]
        b = differ[mate(zmate(m)) * n_req + m]
        return a, a + b, [zneed[deep * m + k] for k in range(deep)]

    most = jnp.int32(0)
    for m in range(n_req):
        _, early, late = pool_of(m)
        extra = sum(late)
        most = jnp.maximum(most, jnp.where(extra > 0, jnp.maximum(1, early) + extra, early))
    best, pool, slots = jnp.int32(len(plans)), jnp.int32(0), jnp.int32(0)
    for k, (c_in, c_out, size) in reversed(list(enumerate(plans))):
        fits = (inside <= c_in) & (outside <= c_out) & (most <= size)
        best = jnp.where(fits, k, best)
        pool = jnp.where(fits, size, pool)
        slots = jnp.where(fits, max(c_in, c_out), slots)
    plan[0] = best

    a, early, late = pool_of(me)
    start = jnp.maximum(1, early)
    near_c, near_d = loc[square + zmate(me) * n_req + me], loc[square + mate(zmate(me)) * n_req + me]
    for k in range(MOST):
        put("pool", k, jnp.where((k == 0) & (a > 0), near_c, near_d))
        put("pool_own", k, flag(k < early))
        where, which = start, jnp.int32(0)
        for j in range(deep):
            which = jnp.where((late[j] > 0) & (k == where), j, which)
            where = where + late[j]
        put("pool_relay", k, which)

    own, near, passed, pools, forward, relay, _ = spots(slots, pool)

    @pl.loop(0, n_req)
    def _(o):
        chip, slot = relayed(me, o)
        _, early, late = pool_of(chip)
        where = jnp.maximum(1, early)
        for j in range(deep):
            where = where + jnp.where(j < slot, late[j], 0)
        na, _, _ = pool_of(o)
        at_far = jnp.where(chip == me, relay + slot, passed + slot)
        at_far = jnp.where(chip == zmate(me), pools + where, at_far)
        at_far = jnp.where(chip == mate(zmate(me)), forward + where, at_far)
        at_near = jnp.where(o == me, own, near)
        at_near = jnp.where(o == zmate(me), pools, at_near)
        at_near = jnp.where(o == mate(zmate(me)), forward + na, at_near)
        at = jnp.where(lax.div(o, half) == lax.div(me, half), at_near, at_far)
        put("at", o, jnp.where(differ[me * n_req + o] > 0, at, 0))


def routes(ids, storage, n_req, blocks, entries, plans):
    place, size = offsets(n_req, blocks)
    square = n_req * n_req
    smem = pl.BlockSpec(memory_space=pltpu.SMEM)
    ints = lambda n: pltpu.SMEM((n,), jnp.int32)
    table, plan = pl.pallas_call(
        functools.partial(route_body, n_req, blocks, entries, plans, place),
        in_specs=[smem, smem],
        out_specs=[smem, smem],
        out_shape=[jax.ShapeDtypeStruct((size,), jnp.int32), jax.ShapeDtypeStruct((1,), jnp.int32)],
        scratch_shapes=[
            ints(square), ints(2 * square + 1), ints(2 * square + 1), ints(square), ints(square),
            ints(square // 2 + 1), ints(n_req), ints(n_req * (n_req // 2) + 1),
        ],
    )(ids, storage)
    return table, plan[0], place


def body(
    n_req, n_tp, slots, pool, place, names, tbl, tok_in, w_in, down_in, up_in, out, *refs
):
    r = types.SimpleNamespace(**dict(zip(names, refs)))
    own, tok, wgt, direct, extra, relay = r.own, r.tok, r.wgt, r.direct, r.extra, r.relay
    half = n_req // 2
    chips = n_tp // 2
    me = lax.axis_index("req")
    tp = lax.axis_index("tp")
    base = (me // half) * half
    mirror = mirror_of(me, n_req)
    inner = (me >= n_req // 4) & (me < n_req - n_req // 4)
    few = jnp.where(inner, slots[0], slots[1])
    mate = me + 1 - 2 * (me % 2)
    zmate = me + 2 - 4 * ((me // 2) % 2)
    at_own, at_near, at_passed, at_pool, at_forward, at_relay, _ = spots(max(slots), pool)
    blocks, _, feat = tok.shape
    cols = wgt.shape[2]
    rank = r.part.shape[3] // 2
    up_rows = own.shape[1] - feat
    chip, core = tp // 2, tp % 2
    tp_mate = tp + 1 - 2 * core

    def near(k):
        return base + lax.rem(me - base + k, half)

    def far(k):
        return (half - base) + lax.rem(me - base + k, half)

    loads = [pltpu.make_async_copy(down_in, own.at[:, pl.ds(0, feat)], r.load_sem.at[0])]
    for c in range(cols // LANES):
        loads.append(
            pltpu.make_async_copy(
                up_in.at[:, :, pl.ds(c * LANES, LANES)],
                own.at[:, pl.ds(feat + c * rank, rank)],
                r.load_sem.at[1 + c],
            )
        )
    tok_load = pltpu.make_async_copy(tok_in, tok, r.load_sem.at[1 + cols // LANES])

    def target(step):
        where = lax.rem(chip + 1 + step % chips, chips)
        return 2 * where + (1 - core if step < chips else core)

    def w_load(step):
        at = pl.multiple_of(target(step) * cols, cols)
        return pltpu.make_async_copy(
            w_in.at[:, pl.ds(at, cols)], wgt.at[step % 2], r.w_sem.at[step]
        )

    for copy in loads:
        copy.start()
    tok_load.start()
    for step in range(2):
        w_load(step).start()

    barrier = pltpu.get_barrier_semaphore()
    for d in range(1, n_req):
        pl.semaphore_signal(
            barrier, inc=1, device_id={"req": lax.rem(me + d, n_req)}, device_id_type=MESH
        )
    for d in range(1, n_tp):
        pl.semaphore_signal(
            barrier, inc=1, device_id={"tp": lax.rem(tp + d, n_tp)}, device_id_type=MESH
        )
    pl.semaphore_wait(barrier, n_req + n_tp - 2)

    def send(src, dst, ss, rs, to):
        return pltpu.make_async_remote_copy(
            src_ref=src, dst_ref=dst, send_sem=ss, recv_sem=rs,
            device_id={"req": to}, device_id_type=MESH,
        )

    def farx_copy(j):
        return send(r.s_farx.at[j], relay.at[j], r.farx_ss.at[j], r.relay_rs.at[j], mirror)

    def near_copy(k):
        return send(
            r.s_near.at[k - 1], direct.at[me], r.near_ss.at[k - 1], r.direct_rs.at[me], near(k)
        )

    def far_copy(k):
        return send(r.s_far.at[k], direct.at[me], r.far_ss.at[k], r.direct_rs.at[me], far(k))

    def got(ref, rs, o):
        send(ref.at[o], ref.at[o], r.core_ss.at[0], rs.at[o], mirror).wait_recv()

    def nearx_copy(k):
        return send(
            r.s_nearx.at[k - 1], extra.at[me], r.nearx_ss.at[k - 1], r.extra_rs.at[me], near(k)
        )

    def relay_copy(k):
        return send(
            r.s_relay.at[k - 1], extra.at[mirror], r.relay_ss.at[k - 1], r.extra_rs.at[mirror],
            near(k),
        )

    def mate_copy():
        return send(r.s_mate, extra.at[at_near], r.mate_ss, r.mate_rs, mate)

    def pool_copy(k):
        return send(
            r.s_pool.at[k], extra.at[at_pool + k], r.pool_ss.at[k], r.pool_rs.at[k], zmate
        )

    def pass_copy(k):
        return send(
            relay.at[k], extra.at[at_passed + k], r.pass_ss.at[k], r.pass_rs.at[k], mate
        )

    def forward_copy(k):
        return send(
            extra.at[at_pool + k], extra.at[at_forward + k], r.forward_ss.at[k],
            r.forward_rs.at[k], mate,
        )

    for copy in loads:
        copy.wait()
    @pl.loop(0, few)
    def _(j):
        r.s_farx[j] = own[tbl[place["far"] + j]]
        farx_copy(j).start()

    if pool:
        r.s_mate[...] = own[tbl[place["extra"] + mate]]
        mate_copy().start()
        r.s_pool[0] = own[tbl[place["pool"]]]
        pool_copy(0).start()

    def start_near():
        @pl.loop(1, half)
        def _(k):
            r.s_near[k - 1] = own[tbl[place["direct"] + near(k)]]
            near_copy(k).start()
            if not pool:
                r.s_nearx[k - 1] = own[tbl[place["extra"] + near(k)]]
                nearx_copy(k).start()

    def start_far(low, high):
        @pl.loop(low, high)
        def _(k):
            r.s_far[k] = own[tbl[place["direct"] + far(k)]]
            far_copy(k).start()

    early = min(EARLY, half) if pool else half
    start_near()
    start_far(0, early)

    direct[me] = own[tbl[place["direct"] + me]]
    extra[at_own if pool else me] = own[tbl[place["extra"] + me]]
    if pool:
        for k in range(1, pool):
            r.s_pool[k] = own[tbl[place["pool"] + k]]

    tok_load.wait()
    tile = 2 if blocks % 2 == 0 else 1

    def product(step, g):
        rows = tok[pl.ds(g * tile, tile)].reshape(tile * BLOCK, feat)
        return jnp.dot(rows, wgt[step % 2], preferred_element_type=jnp.float32)

    def core_copy(q):
        return pltpu.make_async_remote_copy(
            src_ref=r.cs.at[q], dst_ref=r.cr.at[q], send_sem=r.core_ss.at[q],
            recv_sem=r.core_rs.at[q], device_id={"tp": tp_mate}, device_id_type=MESH,
        )

    def x_copy(q):
        to = 2 * lax.rem(chip + 1 + q, chips) + core
        return pltpu.make_async_remote_copy(
            src_ref=r.cr.at[q], dst_ref=r.xr.at[q], send_sem=r.x_ss.at[q], recv_sem=r.x_rs.at[q],
            device_id={"tp": to}, device_id_type=MESH,
        )

    for step in range(n_tp):
        q = step % chips
        w_load(step).wait()
        if step < chips:

            @pl.loop(0, blocks // tile)
            def _(g):
                r.cs[q, pl.ds(g * tile, tile)] = (
                    product(step, g).astype(r.cs.dtype).reshape(tile, BLOCK, cols)
                )

            core_copy(q).start()
        else:
            core_copy(q).wait()

            @pl.loop(0, blocks // tile)
            def _(g):
                at = pl.ds(g * tile, tile)
                mine = product(step, g).reshape(tile, BLOCK, cols)
                r.cr[q, at] = (mine + r.cr[q, at].astype(jnp.float32)).astype(r.cr.dtype)

            if q < chips - 1:
                x_copy(q).start()
        if step + 2 < n_tp:
            w_load(step + 2).start()

    @pl.loop(0, few)
    def _(j):
        farx_copy(j).wait()

    if pool:

        @pl.loop(0, few)
        def _(j):
            pass_copy(j).start()

        for k in range(1, pool):
            r.s_pool[k] = jnp.where(
                tbl[place["pool_own"] + k] > 0,
                r.s_pool[k],
                relay[tbl[place["pool_relay"] + k]],
            )
            pool_copy(k).start()

        @pl.loop(0, few)
        def _(j):
            extra[at_relay + j] = relay[j]

        start_far(early, half)
        for k in range(pool):
            pool_copy(k).wait_recv()
            forward_copy(k).start()
    else:
        extra[mirror] = relay[tbl[place["pick"] + me]]

        @pl.loop(1, half)
        def _(k):
            r.s_relay[k - 1] = relay[tbl[place["pick"] + near(k)]]
            relay_copy(k).start()

    def part_copy(d, o):
        to = lax.rem(tp + d, n_tp)
        return pltpu.make_async_remote_copy(
            src_ref=r.part.at[to // chips, o], dst_ref=r.landed.at[d - 1, o],
            send_sem=r.part_ss.at[d - 1, o], recv_sem=r.part_rs.at[d - 1, o],
            device_id={"tp": to}, device_id_type=MESH,
        )

    def at_extra(o):
        return tbl[place["at"] + o] if pool else o

    def other(o):
        later = tok[tbl[place["blk1"] + o]]
        return jnp.dot(later, extra[at_extra(o), :feat], preferred_element_type=jnp.float32)

    def shrink(o):
        first = tok[tbl[place["blk0"] + o]]
        later = tok[tbl[place["blk1"] + o]]
        differ = tbl[place["differ"] + o] > 0
        one = jnp.dot(first, direct[o, :feat], preferred_element_type=jnp.float32)
        two = jnp.dot(later, direct[o, :feat], preferred_element_type=jnp.float32)
        alt = r.total[o] if pool else other(o).astype(r.total.dtype)
        two = jnp.where(differ, alt, two.astype(r.part.dtype))
        one = one.astype(r.part.dtype)
        r.part[0, o] = jnp.concatenate([one[:, :rank], two[:, :rank]], axis=1)
        r.part[1, o] = jnp.concatenate([one[:, rank:], two[:, rank:]], axis=1)
        for d in range(1, n_tp):
            part_copy(d, o).start()

    if pool:
        mate_copy().wait_recv()

        @pl.loop(0, few)
        def _(j):
            pass_copy(j).wait()

        for k in range(pool):
            forward_copy(k).wait()

        @pl.loop(0, n_req)
        def _(o):
            r.total[o] = other(o).astype(r.total.dtype)

    def finish(o):
        acc = r.part[tp // chips, o].astype(jnp.float32)
        for d in range(1, n_tp):
            part_copy(d, o).wait()
            acc = acc + r.landed[d - 1, o].astype(jnp.float32)
        acc = acc.astype(r.part.dtype)
        up = direct[o, pl.ds(feat, up_rows)]
        alt = extra[at_extra(o), pl.ds(feat, up_rows)]
        alt = jnp.where(tbl[place["differ"] + o] > 0, alt, up)
        for nth, (mine, maps) in enumerate(((acc[:, :rank], up), (acc[:, rank:], alt))):
            for c in range(cols // LANES):
                r.delta[2 * o + nth, :, c * LANES:(c + 1) * LANES] = jnp.dot(
                    mine, maps[c * rank:(c + 1) * rank], preferred_element_type=jnp.float32
                ).astype(r.delta.dtype)

    shrink(me)

    @pl.loop(1, half)
    def _(k):
        o = near(k)
        got(direct, r.direct_rs, o)
        if not pool:
            got(extra, r.extra_rs, o)
        shrink(o)

    @pl.loop(0, half)
    def _(k):
        finish(near(k))

    for q in range(chips - 1):
        x_copy(q).wait()

    def come(k):
        return far(lax.rem(half - k, half))

    @pl.loop(0, half)
    def _(k):
        o = come(k)
        if not pool:

            @pl.when(o != mirror)
            def _():
                got(extra, r.extra_rs, o)

        got(direct, r.direct_rs, o)
        shrink(o)

        @pl.when(k > 0)
        def _():
            finish(come(k - 1))

    finish(come(half - 1))

    @pl.loop(0, blocks)
    def _(b):
        delta = r.delta[2 * tbl[place["own"] + b] + tbl[place["second"] + b]]
        delta = jnp.where(tbl[place["live"] + b] > 0, delta.astype(jnp.float32), 0.0)
        acc = r.cr[chips - 1, b].astype(jnp.float32)
        for q in range(chips - 1):
            acc = acc + r.xr[q, b].astype(jnp.float32)
        r.cr[chips - 1, b] = (acc + delta).astype(r.cr.dtype)

    store = pltpu.make_async_copy(r.cr.at[chips - 1], out, r.out_sem)
    store.start()

    @pl.loop(1, half)
    def _(k):
        near_copy(k).wait_send()
        if not pool:
            nearx_copy(k).wait_send()
            relay_copy(k).wait_send()

    @pl.loop(0, half)
    def _(k):
        far_copy(k).wait_send()

    if pool:
        mate_copy().wait_send()
        for k in range(pool):
            pool_copy(k).wait_send()
    store.wait()


def fused(tbl, tokens, weight, downs, ups, n_req, n_tp, slots, pool, place, ident):
    rows, feat = tokens.shape
    blocks = rows // BLOCK
    entries, _, width = downs.shape
    rank, cols = ups.shape[1:]
    half, chips, most = n_req // 2, n_tp // 2, max(slots)
    kind = tokens.dtype
    slot = (feat + rank * cols // LANES, width)
    tiles = (blocks, BLOCK, cols)
    vmem = lambda *shape: pltpu.VMEM(shape, kind)
    dma = lambda *shape: pltpu.SemaphoreType.DMA(shape)
    one = pltpu.SemaphoreType.DMA
    scratch = dict(
        own=vmem(entries, *slot),
        tok=vmem(blocks, BLOCK, feat),
        wgt=vmem(2, feat, cols),
        s_near=vmem(half - 1, *slot),
        s_far=vmem(half, *slot),
        s_farx=vmem(most, *slot),
        relay=vmem(most, *slot),
        direct=vmem(n_req, *slot),
        cs=vmem(chips, *tiles),
        cr=vmem(chips, *tiles),
        xr=vmem(chips - 1, *tiles),
        part=vmem(2, n_req, BLOCK, width),
        landed=vmem(n_tp - 1, n_req, BLOCK, width),
        total=vmem(n_req, BLOCK, width),
        delta=vmem(2 * n_req, *tiles[1:]),
        load_sem=dma(2 + cols // LANES),
        w_sem=dma(n_tp),
        near_ss=dma(half - 1),
        far_ss=dma(half),
        direct_rs=dma(n_req),
        farx_ss=dma(most),
        relay_rs=dma(most),
        core_ss=dma(chips),
        core_rs=dma(chips),
        x_ss=dma(chips - 1),
        x_rs=dma(chips - 1),
        part_ss=dma(n_tp - 1, n_req),
        part_rs=dma(n_tp - 1, n_req),
        out_sem=one,
    )
    if pool:
        scratch.update(
            extra=vmem(spots(most, pool)[-1], *slot),
            s_mate=vmem(*slot), mate_ss=one, mate_rs=one,
            s_pool=vmem(pool, *slot), pool_ss=dma(pool), pool_rs=dma(pool),
            pass_ss=dma(most), pass_rs=dma(most),
            forward_ss=dma(pool), forward_rs=dma(pool),
        )
    else:
        scratch.update(
            extra=vmem(n_req, *slot), extra_rs=dma(n_req),
            s_nearx=vmem(half - 1, *slot), nearx_ss=dma(half - 1),
            s_relay=vmem(half - 1, *slot), relay_ss=dma(half - 1),
        )
    any_spec = pl.BlockSpec(memory_space=pl.ANY)
    out = pl.pallas_call(
        functools.partial(body, n_req, n_tp, slots, pool, place, tuple(scratch)),
        in_specs=[pl.BlockSpec(memory_space=pltpu.SMEM)] + [any_spec] * 4,
        out_specs=any_spec,
        out_shape=jax.ShapeDtypeStruct(tiles, kind),
        scratch_shapes=list(scratch.values()),
        compiler_params=pltpu.CompilerParams(
            collective_id=ident, has_side_effects=True, vmem_limit_bytes=VMEM_BYTES
        ),
        cost_estimate=pl.CostEstimate(
            flops=2 * rows * feat * (n_tp * cols + width),
            bytes_accessed=4 * rows * feat,
            transcendentals=0,
        ),
    )(tbl, tokens.reshape(blocks, BLOCK, feat), weight, downs, ups)
    return out.reshape(rows, cols)


def per_device(tokens, weight, downs, ups, ids, storage):
    n_req, n_tp = lax.axis_size("req"), lax.axis_size("tp")
    half, blocks = n_req // 2, tokens.shape[0] // BLOCK
    plans = PLANS if n_req == 2 * PLANES else []
    table, plan, place = routes(ids, storage, n_req, blocks, downs.shape[0], plans)
    runs = [
        functools.partial(
            fused, n_req=n_req, n_tp=n_tp, slots=(c_in, c_out), pool=pool, place=place, ident=k
        )
        for k, (c_in, c_out, pool) in enumerate(plans + [(half, half, 0)])
    ]
    return lax.switch(plan, runs, table, tokens, weight, downs, ups)


def solution(mesh):
    placed = (P("req", "tp"), P("tp", None), P("req", "tp", None), P("req", None, "tp"), P(), P())
    return jax.shard_map(
        per_device, mesh=mesh, in_specs=placed, out_specs=P("req", "tp"), check_vma=False
    )
```

```python
import functools
import types

import jax
import jax.numpy as jnp
from jax import lax
from jax.experimental import pallas as pl
from jax.experimental.pallas import tpu as pltpu
from jax.sharding import PartitionSpec as P

BLOCK = 128
LANES = 128
MESH = pl.DeviceIdType.MESH
MOST = 4
PLANS = [
    (1, 1, 2, 2), (1, 2, 2, 1), (2, 1, 3, 0), (2, 2, 3, 0), (2, 3, 3, 0), (3, 2, 3, 0),
]
VMEM_BYTES = 62 * 1024 * 1024


PLANES = 4


def mirror_of(r, n_req):
    wide = n_req // PLANES
    return (PLANES - 1 - r // wide) * wide + r % wide


def offsets(n_req, blocks):
    names = (
        ("direct", n_req), ("extra", n_req), ("far", n_req // 2), ("pick", n_req),
        ("blk0", n_req), ("blk1", n_req), ("differ", n_req),
        ("own", blocks), ("second", blocks), ("live", blocks),
        ("pool", MOST), ("pool_relay", MOST), ("pool_own", MOST), ("at", n_req),
    )
    place, at = {}, 0
    for name, count in names:
        place[name] = at
        at += count
    return place, at


def spots(slots, pool):
    own, near, passed = 0, 1, 2
    pools = passed + slots
    forward = pools + pool
    relayed = forward + pool
    return own, near, passed, pools, forward, relayed, relayed + slots


def route_body(n_req, blocks, entries, plans, place, ids, storage, table, plan, count, loc, blk, differ, rank, listed, amount, zneed):
    half, square = n_req // 2, n_req * n_req
    me = lax.axis_index("req")
    mirror = mirror_of(me, n_req)
    flag = lambda c: jnp.where(c, 1, 0).astype(jnp.int32)

    def put(name, k, value):
        table[place[name] + k] = value

    @pl.loop(0, square)
    def _(k):
        count[k] = 0
        loc[k] = 0
        loc[square + k] = 0
        blk[k] = 0
        blk[square + k] = 0
        rank[k] = 0

    def entry_of(k):
        ident = ids[k]
        entry = storage[jnp.maximum(ident - 1, 0)]
        return ident > 0, lax.div(entry, entries), lax.rem(entry, entries)

    @pl.loop(0, n_req)
    def _(i):
        for b in range(blocks):
            live, o, l = entry_of(i * blocks + b)
            at = i * n_req + o
            nth = count[at]
            count[at] = nth + flag(live)
            spot = jnp.where(live, nth * square + at, 2 * square)
            loc[spot] = l
            blk[spot] = b

    @pl.loop(0, n_req)
    def _(o):
        base = lax.div(o, half) * half
        ats = [(half - base + e) * n_req + o for e in range(half)]
        for e in range(half):
            at = (base + e) * n_req + o
            differ[at] = flag((count[at] == 2) & (loc[at] != loc[square + at]))
        a0 = [loc[at] for at in ats]
        a1 = [loc[square + at] for at in ats]
        two = [(count[at] == 2) & (x != y) for at, x, y in zip(ats, a0, a1)]
        names = lambda e, a: flag(two[e] & ((a0[e] == a) | (a1[e] == a)))
        used = jnp.int32(0)
        chosen, ranks = [], []
        for e, at in enumerate(ats):
            score0 = sum(names(f, a0[e]) for f in range(half)) * entries - a0[e]
            score1 = sum(names(f, a1[e]) for f in range(half)) * entries - a1[e]
            swap = two[e] & (score0 > score1)
            x = jnp.where(swap, a0[e], a1[e])
            loc[at] = jnp.where(swap, a1[e], a0[e])
            loc[square + at] = x
            b0, b1 = blk[at], blk[square + at]
            blk[at] = jnp.where(swap, b1, b0)
            blk[square + at] = jnp.where(swap, b0, b1)
            differ[at] = flag(two[e])
            mine, new = used, two[e]
            for f in range(e):
                same = two[e] & two[f] & (chosen[f] == x)
                mine = jnp.where(same, ranks[f], mine)
                new = new & jnp.logical_not(same)
            rank[at] = jnp.where(two[e], mine, 0)
            listed[jnp.where(new, o * half + mine, n_req * half)] = x
            used = used + flag(new)
            chosen.append(x)
            ranks.append(mine)
        amount[o] = used

    @pl.loop(0, n_req)
    def _(k):
        put("direct", k, loc[k * n_req + me])
        put("extra", k, loc[square + k * n_req + me])
        put("pick", k, rank[k * n_req + mirror])
        put("blk0", k, blk[me * n_req + k])
        put("blk1", k, blk[square + me * n_req + k])
        put("differ", k, differ[me * n_req + k])

    for k in range(half):
        put("far", k, jnp.where(k < amount[me], listed[me * half + k], 0))

    for b in range(blocks):
        live, o, _ = entry_of(me * blocks + b)
        at = me * n_req + o
        second = flag(live & (blk[at] != b))
        put("own", b, o)
        put("second", b, second)
        put("live", b, flag(live))

    plan[0] = len(plans)
    if not plans:
        return
    mate = lambda r: r + 1 - 2 * lax.rem(r, 2)
    zmate = lambda r: r + 2 - 4 * lax.rem(lax.div(r, 2), 2)
    need = []
    for p in range(PLANES):
        x, y = amount[2 * p], amount[2 * p + 1]
        need.append(jnp.maximum(jnp.maximum(x, y), 1))
    inside, outside = jnp.maximum(need[1], need[2]), jnp.maximum(need[0], need[3])

    deep = max(max(c_in, c_out) for c_in, c_out, _, _ in plans)
    for k in range(deep * n_req + 1):
        zneed[k] = 0

    def relayed(i, o):
        return mirror_of(o, n_req), rank[i * n_req + o]

    @pl.loop(0, n_req)
    def _(o):
        base = lax.div(o, half) * half
        for e in range(half):
            i = half - base + e
            chip, slot = relayed(i, o)
            want = (differ[i * n_req + o] > 0) & (lax.div(i, 2) != lax.div(chip, 2))
            zneed[jnp.where(want & (slot < deep), deep * chip + slot, deep * n_req)] = 1

    def pool_of(m):
        a = differ[zmate(m) * n_req + m]
        b = differ[mate(zmate(m)) * n_req + m]
        return a, a + b, [zneed[deep * m + k] for k in range(deep)]

    most = jnp.int32(0)
    for m in range(n_req):
        _, early, late = pool_of(m)
        extra = sum(late)
        most = jnp.maximum(most, jnp.where(extra > 0, jnp.maximum(1, early) + extra, early))
    best, pool, slots = jnp.int32(len(plans)), jnp.int32(0), jnp.int32(0)
    for k, (c_in, c_out, size, _) in reversed(list(enumerate(plans))):
        fits = (inside <= c_in) & (outside <= c_out) & (most <= size)
        best = jnp.where(fits, k, best)
        pool = jnp.where(fits, size, pool)
        slots = jnp.where(fits, max(c_in, c_out), slots)
    plan[0] = best

    a, early, late = pool_of(me)
    start = jnp.maximum(1, early)
    near_c, near_d = loc[square + zmate(me) * n_req + me], loc[square + mate(zmate(me)) * n_req + me]
    for k in range(MOST):
        put("pool", k, jnp.where((k == 0) & (a > 0), near_c, near_d))
        put("pool_own", k, flag(k < early))
        where, which = start, jnp.int32(0)
        for j in range(deep):
            which = jnp.where((late[j] > 0) & (k == where), j, which)
            where = where + late[j]
        put("pool_relay", k, which)

    own, near, passed, pools, forward, relay, _ = spots(slots, pool)

    @pl.loop(0, n_req)
    def _(o):
        chip, slot = relayed(me, o)
        _, early, late = pool_of(chip)
        where = jnp.maximum(1, early)
        for j in range(deep):
            where = where + jnp.where(j < slot, late[j], 0)
        na, _, _ = pool_of(o)
        at_far = jnp.where(chip == me, relay + slot, passed + slot)
        at_far = jnp.where(chip == zmate(me), pools + where, at_far)
        at_far = jnp.where(chip == mate(zmate(me)), forward + where, at_far)
        at_near = jnp.where(o == me, own, near)
        at_near = jnp.where(o == zmate(me), pools, at_near)
        at_near = jnp.where(o == mate(zmate(me)), forward + na, at_near)
        at = jnp.where(lax.div(o, half) == lax.div(me, half), at_near, at_far)
        put("at", o, jnp.where(differ[me * n_req + o] > 0, at, 0))


def routes(ids, storage, n_req, blocks, entries, plans):
    place, size = offsets(n_req, blocks)
    square = n_req * n_req
    smem = pl.BlockSpec(memory_space=pltpu.SMEM)
    ints = lambda n: pltpu.SMEM((n,), jnp.int32)
    table, plan = pl.pallas_call(
        functools.partial(route_body, n_req, blocks, entries, plans, place),
        in_specs=[smem, smem],
        out_specs=[smem, smem],
        out_shape=[jax.ShapeDtypeStruct((size,), jnp.int32), jax.ShapeDtypeStruct((1,), jnp.int32)],
        scratch_shapes=[
            ints(square), ints(2 * square + 1), ints(2 * square + 1), ints(square), ints(square),
            ints(square // 2 + 1), ints(n_req), ints(n_req * (n_req // 2) + 1),
        ],
    )(ids, storage)
    return table, plan[0], place


def body(
    n_req, n_tp, slots, pool, first, place, names, tbl, tok_in, w_in, down_in, up_in, out, *refs
):
    r = types.SimpleNamespace(**dict(zip(names, refs)))
    own, tok, wgt, direct, extra, relay = r.own, r.tok, r.wgt, r.direct, r.extra, r.relay
    half = n_req // 2
    chips = n_tp // 2
    me = lax.axis_index("req")
    tp = lax.axis_index("tp")
    base = (me // half) * half
    mirror = mirror_of(me, n_req)
    inner = (me >= n_req // 4) & (me < n_req - n_req // 4)
    few = jnp.where(inner, slots[0], slots[1])
    mate = me + 1 - 2 * (me % 2)
    zmate = me + 2 - 4 * ((me // 2) % 2)
    at_own, at_near, at_passed, at_pool, at_forward, at_relay, _ = spots(max(slots), pool)
    blocks, _, feat = tok.shape
    cols = wgt.shape[2]
    rank = r.part.shape[3] // 2
    up_rows = own.shape[1] - feat
    chip, core = tp // 2, tp % 2
    tp_mate = tp + 1 - 2 * core

    def near(k):
        return base + lax.rem(me - base + k, half)

    def far(k):
        return (half - base) + lax.rem(me - base + k, half)

    loads = [pltpu.make_async_copy(down_in, own.at[:, pl.ds(0, feat)], r.load_sem.at[0])]
    for c in range(cols // LANES):
        loads.append(
            pltpu.make_async_copy(
                up_in.at[:, :, pl.ds(c * LANES, LANES)],
                own.at[:, pl.ds(feat + c * rank, rank)],
                r.load_sem.at[1 + c],
            )
        )
    tok_load = pltpu.make_async_copy(tok_in, tok, r.load_sem.at[1 + cols // LANES])

    def target(step):
        where = lax.rem(chip + 1 + lax.rem(step, chips), chips)
        return 2 * where + jnp.where(step < chips, 1 - core, core)

    def w_load(step):
        at = pl.multiple_of(target(step) * cols, cols)
        return pltpu.make_async_copy(
            w_in.at[:, pl.ds(at, cols)], wgt.at[lax.rem(step, 2)], r.w_sem.at[step]
        )

    for copy in loads:
        copy.start()
    tok_load.start()
    for step in range(2):
        w_load(step).start()

    barrier = pltpu.get_barrier_semaphore()
    for d in range(1, n_req):
        pl.semaphore_signal(
            barrier, inc=1, device_id={"req": lax.rem(me + d, n_req)}, device_id_type=MESH
        )
    for d in range(1, n_tp):
        pl.semaphore_signal(
            barrier, inc=1, device_id={"tp": lax.rem(tp + d, n_tp)}, device_id_type=MESH
        )
    pl.semaphore_wait(barrier, n_req + n_tp - 2)

    def send(src, dst, ss, rs, to):
        return pltpu.make_async_remote_copy(
            src_ref=src, dst_ref=dst, send_sem=ss, recv_sem=rs,
            device_id={"req": to}, device_id_type=MESH,
        )

    def farx_copy(j):
        return send(r.s_farx.at[j], relay.at[j], r.farx_ss.at[j], r.relay_rs.at[j], mirror)

    def near_copy(k):
        return send(
            r.s_near.at[k - 1], direct.at[me], r.near_ss.at[k - 1], r.direct_rs.at[me], near(k)
        )

    def far_copy(k):
        return send(r.s_far.at[k], direct.at[me], r.far_ss.at[k], r.direct_rs.at[me], far(k))

    def got(ref, rs, o):
        send(ref.at[o], ref.at[o], r.core_ss.at[0], rs.at[o], mirror).wait_recv()

    def nearx_copy(k):
        return send(
            r.s_nearx.at[k - 1], extra.at[me], r.nearx_ss.at[k - 1], r.extra_rs.at[me], near(k)
        )

    def relay_copy(k):
        return send(
            r.s_relay.at[k - 1], extra.at[mirror], r.relay_ss.at[k - 1], r.extra_rs.at[mirror],
            near(k),
        )

    def mate_copy():
        return send(r.s_mate, extra.at[at_near], r.mate_ss, r.mate_rs, mate)

    def pool_copy(k):
        return send(
            r.s_pool.at[k], extra.at[at_pool + k], r.pool_ss.at[k], r.pool_rs.at[k], zmate
        )

    def pass_copy(k):
        return send(
            relay.at[k], extra.at[at_passed + k], r.pass_ss.at[k], r.pass_rs.at[k], mate
        )

    def forward_copy(k):
        return send(
            extra.at[at_pool + k], extra.at[at_forward + k], r.forward_ss.at[k],
            r.forward_rs.at[k], mate,
        )

    for copy in loads:
        copy.wait()
    @pl.loop(0, few)
    def _(j):
        r.s_farx[j] = own[tbl[place["far"] + j]]
        farx_copy(j).start()

    if pool:
        r.s_mate[...] = own[tbl[place["extra"] + mate]]
        mate_copy().start()
        r.s_pool[0] = own[tbl[place["pool"]]]
        pool_copy(0).start()

    def start_near():
        @pl.loop(1, half)
        def _(k):
            r.s_near[k - 1] = own[tbl[place["direct"] + near(k)]]
            near_copy(k).start()
            if not pool:
                r.s_nearx[k - 1] = own[tbl[place["extra"] + near(k)]]
                nearx_copy(k).start()

    def start_far(low, high):
        @pl.loop(low, high)
        def _(k):
            r.s_far[k] = own[tbl[place["direct"] + far(k)]]
            far_copy(k).start()

    early = first if pool else half
    start_near()
    start_far(0, early)

    direct[me] = own[tbl[place["direct"] + me]]
    extra[at_own if pool else me] = own[tbl[place["extra"] + me]]
    if pool:
        for k in range(1, pool):
            r.s_pool[k] = own[tbl[place["pool"] + k]]

    tok_load.wait()
    tile = 2 if blocks % 2 == 0 else 1

    def product(step, g):
        rows = tok[pl.ds(g * tile, tile)].reshape(tile * BLOCK, feat)
        return jnp.dot(rows, wgt[lax.rem(step, 2)], preferred_element_type=jnp.float32)

    def core_copy(q):
        return pltpu.make_async_remote_copy(
            src_ref=r.cs.at[q], dst_ref=r.cr.at[q], send_sem=r.core_ss.at[q],
            recv_sem=r.core_rs.at[q], device_id={"tp": tp_mate}, device_id_type=MESH,
        )

    def x_copy(q):
        to = 2 * lax.rem(chip + 1 + q, chips) + core
        return pltpu.make_async_remote_copy(
            src_ref=r.cr.at[q], dst_ref=r.xr.at[q], send_sem=r.x_ss.at[q], recv_sem=r.x_rs.at[q],
            device_id={"tp": to}, device_id_type=MESH,
        )

    @pl.loop(0, n_tp)
    def _(step):
        q = lax.rem(step, chips)
        w_load(step).wait()

        @pl.when(step < chips)
        def _():
            @pl.loop(0, blocks // tile)
            def _(g):
                r.cs[q, pl.ds(g * tile, tile)] = (
                    product(step, g).astype(r.cs.dtype).reshape(tile, BLOCK, cols)
                )

            core_copy(q).start()

        @pl.when(step >= chips)
        def _():
            core_copy(q).wait()

            @pl.loop(0, blocks // tile)
            def _(g):
                at = pl.ds(g * tile, tile)
                mine = product(step, g).reshape(tile, BLOCK, cols)
                r.cr[q, at] = (mine + r.cr[q, at].astype(jnp.float32)).astype(r.cr.dtype)

            @pl.when(q < chips - 1)
            def _():
                x_copy(q).start()

        @pl.when(step + 2 < n_tp)
        def _():
            w_load(step + 2).start()

    @pl.loop(0, few)
    def _(j):
        farx_copy(j).wait()

    if pool:

        @pl.loop(0, few)
        def _(j):
            pass_copy(j).start()

        for k in range(1, pool):
            r.s_pool[k] = jnp.where(
                tbl[place["pool_own"] + k] > 0,
                r.s_pool[k],
                relay[tbl[place["pool_relay"] + k]],
            )
            pool_copy(k).start()

        @pl.loop(0, few)
        def _(j):
            extra[at_relay + j] = relay[j]

        start_far(early, half)
        for k in range(pool):
            pool_copy(k).wait_recv()
            forward_copy(k).start()
    else:
        extra[mirror] = relay[tbl[place["pick"] + me]]

        @pl.loop(1, half)
        def _(k):
            r.s_relay[k - 1] = relay[tbl[place["pick"] + near(k)]]
            relay_copy(k).start()

    def part_copy(d, o):
        to = lax.rem(tp + d, n_tp)
        return pltpu.make_async_remote_copy(
            src_ref=r.part.at[to // chips, o], dst_ref=r.landed.at[d - 1, o],
            send_sem=r.part_ss.at[d - 1, o], recv_sem=r.part_rs.at[d - 1, o],
            device_id={"tp": to}, device_id_type=MESH,
        )

    def at_extra(o):
        return tbl[place["at"] + o] if pool else o

    def other(o):
        later = tok[tbl[place["blk1"] + o]]
        return jnp.dot(later, extra[at_extra(o), :feat], preferred_element_type=jnp.float32)

    def shrink(o):
        first = tok[tbl[place["blk0"] + o]]
        later = tok[tbl[place["blk1"] + o]]
        differ = tbl[place["differ"] + o] > 0
        one = jnp.dot(first, direct[o, :feat], preferred_element_type=jnp.float32)
        two = jnp.dot(later, direct[o, :feat], preferred_element_type=jnp.float32)
        alt = r.total[o] if pool else other(o).astype(r.total.dtype)
        two = jnp.where(differ, alt, two.astype(r.part.dtype))
        one = one.astype(r.part.dtype)
        r.part[0, o] = jnp.concatenate([one[:, :rank], two[:, :rank]], axis=1)
        r.part[1, o] = jnp.concatenate([one[:, rank:], two[:, rank:]], axis=1)
        for d in range(1, n_tp):
            part_copy(d, o).start()

    if pool:
        mate_copy().wait_recv()

        @pl.loop(0, few)
        def _(j):
            pass_copy(j).wait()

        for k in range(pool):
            forward_copy(k).wait()

        @pl.loop(0, n_req)
        def _(o):
            r.total[o] = other(o).astype(r.total.dtype)

    def finish(o):
        acc = r.part[tp // chips, o].astype(jnp.float32)
        for d in range(1, n_tp):
            part_copy(d, o).wait()
            acc = acc + r.landed[d - 1, o].astype(jnp.float32)
        acc = acc.astype(r.part.dtype)
        up = direct[o, pl.ds(feat, up_rows)]
        alt = extra[at_extra(o), pl.ds(feat, up_rows)]
        alt = jnp.where(tbl[place["differ"] + o] > 0, alt, up)
        for nth, (mine, maps) in enumerate(((acc[:, :rank], up), (acc[:, rank:], alt))):
            for c in range(cols // LANES):
                r.delta[2 * o + nth, :, c * LANES:(c + 1) * LANES] = jnp.dot(
                    mine, maps[c * rank:(c + 1) * rank], preferred_element_type=jnp.float32
                ).astype(r.delta.dtype)

    def nth_owner(k):
        return jnp.where(k < half, near(k), far(lax.rem(n_req - k, half)))

    @pl.loop(0, n_req + 1)
    def _(k):
        @pl.when(k < n_req)
        def _():
            o = nth_owner(k)

            @pl.when(k > 0)
            def _():
                got(direct, r.direct_rs, o)

            if not pool:

                @pl.when((k > 0) & (o != mirror))
                def _():
                    got(extra, r.extra_rs, o)

            shrink(o)

        @pl.when(k > 0)
        def _():
            finish(nth_owner(k - 1))

    for q in range(chips - 1):
        x_copy(q).wait()

    @pl.loop(0, blocks)
    def _(b):
        delta = r.delta[2 * tbl[place["own"] + b] + tbl[place["second"] + b]]
        delta = jnp.where(tbl[place["live"] + b] > 0, delta.astype(jnp.float32), 0.0)
        acc = r.cr[chips - 1, b].astype(jnp.float32)
        for q in range(chips - 1):
            acc = acc + r.xr[q, b].astype(jnp.float32)
        r.cr[chips - 1, b] = (acc + delta).astype(r.cr.dtype)

    store = pltpu.make_async_copy(r.cr.at[chips - 1], out, r.out_sem)
    store.start()

    @pl.loop(1, half)
    def _(k):
        near_copy(k).wait_send()
        if not pool:
            nearx_copy(k).wait_send()
            relay_copy(k).wait_send()

    @pl.loop(0, half)
    def _(k):
        far_copy(k).wait_send()

    if pool:
        mate_copy().wait_send()
        for k in range(pool):
            pool_copy(k).wait_send()
    store.wait()


def fused(
    tbl, tokens, weight, downs, ups, n_req, n_tp, slots, pool, first, place, ident
):
    rows, feat = tokens.shape
    blocks = rows // BLOCK
    entries, _, width = downs.shape
    rank, cols = ups.shape[1:]
    half, chips, most = n_req // 2, n_tp // 2, max(slots)
    kind = tokens.dtype
    slot = (feat + rank * cols // LANES, width)
    tiles = (blocks, BLOCK, cols)
    vmem = lambda *shape: pltpu.VMEM(shape, kind)
    dma = lambda *shape: pltpu.SemaphoreType.DMA(shape)
    one = pltpu.SemaphoreType.DMA
    scratch = dict(
        own=vmem(entries, *slot),
        tok=vmem(blocks, BLOCK, feat),
        wgt=vmem(2, feat, cols),
        s_near=vmem(half - 1, *slot),
        s_far=vmem(half, *slot),
        s_farx=vmem(most, *slot),
        relay=vmem(most, *slot),
        direct=vmem(n_req, *slot),
        cs=vmem(chips, *tiles),
        cr=vmem(chips, *tiles),
        xr=vmem(chips - 1, *tiles),
        part=vmem(2, n_req, BLOCK, width),
        landed=vmem(n_tp - 1, n_req, BLOCK, width),
        total=vmem(n_req, BLOCK, width),
        delta=vmem(2 * n_req, *tiles[1:]),
        load_sem=dma(2 + cols // LANES),
        w_sem=dma(n_tp),
        near_ss=dma(half - 1),
        far_ss=dma(half),
        direct_rs=dma(n_req),
        farx_ss=dma(most),
        relay_rs=dma(most),
        core_ss=dma(chips),
        core_rs=dma(chips),
        x_ss=dma(chips - 1),
        x_rs=dma(chips - 1),
        part_ss=dma(n_tp - 1, n_req),
        part_rs=dma(n_tp - 1, n_req),
        out_sem=one,
    )
    if pool:
        scratch.update(
            extra=vmem(spots(most, pool)[-1], *slot),
            s_mate=vmem(*slot), mate_ss=one, mate_rs=one,
            s_pool=vmem(pool, *slot), pool_ss=dma(pool), pool_rs=dma(pool),
            pass_ss=dma(most), pass_rs=dma(most),
            forward_ss=dma(pool), forward_rs=dma(pool),
        )
    else:
        scratch.update(
            extra=vmem(n_req, *slot), extra_rs=dma(n_req),
            s_nearx=vmem(half - 1, *slot), nearx_ss=dma(half - 1),
            s_relay=vmem(half - 1, *slot), relay_ss=dma(half - 1),
        )
    any_spec = pl.BlockSpec(memory_space=pl.ANY)
    out = pl.pallas_call(
        functools.partial(body, n_req, n_tp, slots, pool, first, place, tuple(scratch)),
        in_specs=[pl.BlockSpec(memory_space=pltpu.SMEM)] + [any_spec] * 4,
        out_specs=any_spec,
        out_shape=jax.ShapeDtypeStruct(tiles, kind),
        scratch_shapes=list(scratch.values()),
        compiler_params=pltpu.CompilerParams(
            collective_id=ident, has_side_effects=True, vmem_limit_bytes=VMEM_BYTES
        ),
        cost_estimate=pl.CostEstimate(
            flops=2 * rows * feat * (n_tp * cols + width),
            bytes_accessed=4 * rows * feat,
            transcendentals=0,
        ),
    )(tbl, tokens.reshape(blocks, BLOCK, feat), weight, downs, ups)
    return out.reshape(rows, cols)


def per_device(tokens, weight, downs, ups, ids, storage):
    n_req, n_tp = lax.axis_size("req"), lax.axis_size("tp")
    half, blocks = n_req // 2, tokens.shape[0] // BLOCK
    plans = PLANS if n_req == 2 * PLANES else []
    table, plan, place = routes(ids, storage, n_req, blocks, downs.shape[0], plans)
    runs = [
        functools.partial(
            fused, n_req=n_req, n_tp=n_tp, slots=(c_in, c_out), pool=pool, first=first,
            place=place, ident=k,
        )
        for k, (c_in, c_out, pool, first) in enumerate(plans + [(half, half, 0, 0)])
    ]
    return lax.switch(plan, runs, table, tokens, weight, downs, ups)


def solution(mesh):
    placed = (P("req", "tp"), P("tp", None), P("req", "tp", None), P("req", None, "tp"), P(), P())
    return jax.shard_map(
        per_device, mesh=mesh, in_specs=placed, out_specs=P("req", "tp"), check_vma=False
    )
```

```python
import functools
import types

import jax
import jax.numpy as jnp
from jax import lax
from jax.experimental import pallas as pl
from jax.experimental.pallas import tpu as pltpu
from jax.sharding import PartitionSpec as P

BLOCK = 128
LANES = 128
MESH = pl.DeviceIdType.MESH
MOST = 4
PLANS = [
    (1, 1, 2, 2), (1, 2, 2, 1), (2, 1, 3, 0), (2, 2, 3, 0), (2, 3, 3, 0), (3, 2, 3, 0),
]
VMEM_BYTES = 62 * 1024 * 1024


PLANES = 4


def mirror_of(r, n_req):
    wide = n_req // PLANES
    return (PLANES - 1 - r // wide) * wide + r % wide


def offsets(n_req, blocks):
    names = (
        ("direct", n_req), ("extra", n_req), ("far", n_req // 2), ("pick", n_req),
        ("blk0", n_req), ("blk1", n_req), ("differ", n_req),
        ("own", blocks), ("second", blocks), ("live", blocks),
        ("pool", MOST), ("pool_relay", MOST), ("pool_own", MOST), ("at", n_req),
    )
    place, at = {}, 0
    for name, count in names:
        place[name] = at
        at += count
    return place, at


def spots(slots, pool):
    own, near, passed = 0, 1, 2
    pools = passed + slots
    forward = pools + pool
    relayed = forward + pool
    return own, near, passed, pools, forward, relayed, relayed + slots


def route_body(n_req, blocks, entries, plans, place, ids, storage, table, plan, count, loc, blk, differ, rank, listed, amount, zneed):
    half, square = n_req // 2, n_req * n_req
    me = lax.axis_index("req")
    mirror = mirror_of(me, n_req)
    flag = lambda c: jnp.where(c, 1, 0).astype(jnp.int32)

    def put(name, k, value):
        table[place[name] + k] = value

    @pl.loop(0, square)
    def _(k):
        count[k] = 0
        loc[k] = 0
        loc[square + k] = 0
        blk[k] = 0
        blk[square + k] = 0
        rank[k] = 0

    def entry_of(k):
        ident = ids[k]
        entry = storage[jnp.maximum(ident - 1, 0)]
        return ident > 0, lax.div(entry, entries), lax.rem(entry, entries)

    @pl.loop(0, n_req)
    def _(i):
        for b in range(blocks):
            live, o, l = entry_of(i * blocks + b)
            at = i * n_req + o
            nth = count[at]
            count[at] = nth + flag(live)
            spot = jnp.where(live, nth * square + at, 2 * square)
            loc[spot] = l
            blk[spot] = b

    @pl.loop(0, n_req)
    def _(o):
        base = lax.div(o, half) * half
        ats = [(half - base + e) * n_req + o for e in range(half)]
        for e in range(half):
            at = (base + e) * n_req + o
            differ[at] = flag((count[at] == 2) & (loc[at] != loc[square + at]))
        a0 = [loc[at] for at in ats]
        a1 = [loc[square + at] for at in ats]
        two = [(count[at] == 2) & (x != y) for at, x, y in zip(ats, a0, a1)]
        names = lambda e, a: flag(two[e] & ((a0[e] == a) | (a1[e] == a)))
        used = jnp.int32(0)
        chosen, ranks = [], []
        for e, at in enumerate(ats):
            score0 = sum(names(f, a0[e]) for f in range(half)) * entries - a0[e]
            score1 = sum(names(f, a1[e]) for f in range(half)) * entries - a1[e]
            swap = two[e] & (score0 > score1)
            x = jnp.where(swap, a0[e], a1[e])
            loc[at] = jnp.where(swap, a1[e], a0[e])
            loc[square + at] = x
            b0, b1 = blk[at], blk[square + at]
            blk[at] = jnp.where(swap, b1, b0)
            blk[square + at] = jnp.where(swap, b0, b1)
            differ[at] = flag(two[e])
            mine, new = used, two[e]
            for f in range(e):
                same = two[e] & two[f] & (chosen[f] == x)
                mine = jnp.where(same, ranks[f], mine)
                new = new & jnp.logical_not(same)
            rank[at] = jnp.where(two[e], mine, 0)
            listed[jnp.where(new, o * half + mine, n_req * half)] = x
            used = used + flag(new)
            chosen.append(x)
            ranks.append(mine)
        amount[o] = used

    @pl.loop(0, n_req)
    def _(k):
        put("direct", k, loc[k * n_req + me])
        put("extra", k, loc[square + k * n_req + me])
        put("pick", k, rank[k * n_req + mirror])
        put("blk0", k, blk[me * n_req + k])
        put("blk1", k, blk[square + me * n_req + k])
        put("differ", k, differ[me * n_req + k])

    for k in range(half):
        put("far", k, jnp.where(k < amount[me], listed[me * half + k], 0))

    for b in range(blocks):
        live, o, _ = entry_of(me * blocks + b)
        at = me * n_req + o
        second = flag(live & (blk[at] != b))
        put("own", b, o)
        put("second", b, second)
        put("live", b, flag(live))

    plan[0] = len(plans)
    if not plans:
        return
    mate = lambda r: r + 1 - 2 * lax.rem(r, 2)
    zmate = lambda r: r + 2 - 4 * lax.rem(lax.div(r, 2), 2)
    need = []
    for p in range(PLANES):
        x, y = amount[2 * p], amount[2 * p + 1]
        need.append(jnp.maximum(jnp.maximum(x, y), 1))
    inside, outside = jnp.maximum(need[1], need[2]), jnp.maximum(need[0], need[3])

    deep = max(max(c_in, c_out) for c_in, c_out, _, _ in plans)
    for k in range(deep * n_req + 1):
        zneed[k] = 0

    def relayed(i, o):
        return mirror_of(o, n_req), rank[i * n_req + o]

    @pl.loop(0, n_req)
    def _(o):
        base = lax.div(o, half) * half
        for e in range(half):
            i = half - base + e
            chip, slot = relayed(i, o)
            want = (differ[i * n_req + o] > 0) & (lax.div(i, 2) != lax.div(chip, 2))
            zneed[jnp.where(want & (slot < deep), deep * chip + slot, deep * n_req)] = 1

    def pool_of(m):
        a = differ[zmate(m) * n_req + m]
        b = differ[mate(zmate(m)) * n_req + m]
        return a, a + b, [zneed[deep * m + k] for k in range(deep)]

    most = jnp.int32(0)
    for m in range(n_req):
        _, early, late = pool_of(m)
        extra = sum(late)
        most = jnp.maximum(most, jnp.where(extra > 0, jnp.maximum(1, early) + extra, early))
    best, pool, slots = jnp.int32(len(plans)), jnp.int32(0), jnp.int32(0)
    for k, (c_in, c_out, size, _) in reversed(list(enumerate(plans))):
        fits = (inside <= c_in) & (outside <= c_out) & (most <= size)
        best = jnp.where(fits, k, best)
        pool = jnp.where(fits, size, pool)
        slots = jnp.where(fits, max(c_in, c_out), slots)
    plan[0] = best

    a, early, late = pool_of(me)
    start = jnp.maximum(1, early)
    near_c, near_d = loc[square + zmate(me) * n_req + me], loc[square + mate(zmate(me)) * n_req + me]
    for k in range(MOST):
        put("pool", k, jnp.where((k == 0) & (a > 0), near_c, near_d))
        put("pool_own", k, flag(k < early))
        where, which = start, jnp.int32(0)
        for j in range(deep):
            which = jnp.where((late[j] > 0) & (k == where), j, which)
            where = where + late[j]
        put("pool_relay", k, which)

    own, near, passed, pools, forward, relay, _ = spots(slots, pool)

    @pl.loop(0, n_req)
    def _(o):
        chip, slot = relayed(me, o)
        _, early, late = pool_of(chip)
        where = jnp.maximum(1, early)
        for j in range(deep):
            where = where + jnp.where(j < slot, late[j], 0)
        na, _, _ = pool_of(o)
        at_far = jnp.where(chip == me, relay + slot, passed + slot)
        at_far = jnp.where(chip == zmate(me), pools + where, at_far)
        at_far = jnp.where(chip == mate(zmate(me)), forward + where, at_far)
        at_near = jnp.where(o == me, own, near)
        at_near = jnp.where(o == zmate(me), pools, at_near)
        at_near = jnp.where(o == mate(zmate(me)), forward + na, at_near)
        at = jnp.where(lax.div(o, half) == lax.div(me, half), at_near, at_far)
        put("at", o, jnp.where(differ[me * n_req + o] > 0, at, 0))


def routes(ids, storage, n_req, blocks, entries, plans):
    place, size = offsets(n_req, blocks)
    square = n_req * n_req
    smem = pl.BlockSpec(memory_space=pltpu.SMEM)
    ints = lambda n: pltpu.SMEM((n,), jnp.int32)
    table, plan = pl.pallas_call(
        functools.partial(route_body, n_req, blocks, entries, plans, place),
        in_specs=[smem, smem],
        out_specs=[smem, smem],
        out_shape=[jax.ShapeDtypeStruct((size,), jnp.int32), jax.ShapeDtypeStruct((1,), jnp.int32)],
        scratch_shapes=[
            ints(square), ints(2 * square + 1), ints(2 * square + 1), ints(square), ints(square),
            ints(square // 2 + 1), ints(n_req), ints(n_req * (n_req // 2) + 1),
        ],
    )(ids, storage)
    return table, plan[0], place


def body(
    n_req, n_tp, slots, pool, first, place, names, tbl, tok_in, w_in, down_in, up_in, out, *refs
):
    r = types.SimpleNamespace(**dict(zip(names, refs)))
    own, tok, wgt, direct, extra, relay = r.own, r.tok, r.wgt, r.direct, r.extra, r.relay
    half = n_req // 2
    chips = n_tp // 2
    me = lax.axis_index("req")
    tp = lax.axis_index("tp")
    base = (me // half) * half
    mirror = mirror_of(me, n_req)
    inner = (me >= n_req // 4) & (me < n_req - n_req // 4)
    few = jnp.where(inner, slots[0], slots[1])
    mate = me + 1 - 2 * (me % 2)
    zmate = me + 2 - 4 * ((me // 2) % 2)
    at_own, at_near, at_passed, at_pool, at_forward, at_relay, _ = spots(max(slots), pool)
    blocks, _, feat = tok.shape
    cols = wgt.shape[2]
    rank = r.part.shape[3] // 2
    up_rows = own.shape[1] - feat
    chip, core = tp // 2, tp % 2
    tp_mate = tp + 1 - 2 * core

    def near(k):
        return base + lax.rem(me - base + k, half)

    def far(k):
        return (half - base) + lax.rem(me - base + k, half)

    loads = [pltpu.make_async_copy(down_in, own.at[:, pl.ds(0, feat)], r.load_sem.at[0])]
    for c in range(cols // LANES):
        loads.append(
            pltpu.make_async_copy(
                up_in.at[:, :, pl.ds(c * LANES, LANES)],
                own.at[:, pl.ds(feat + c * rank, rank)],
                r.load_sem.at[1 + c],
            )
        )
    tok_load = pltpu.make_async_copy(tok_in, tok, r.load_sem.at[1 + cols // LANES])

    def target(step):
        where = lax.rem(chip + 1 + lax.rem(step, chips), chips)
        return 2 * where + jnp.where(step < chips, 1 - core, core)

    def w_load(step):
        at = pl.multiple_of(target(step) * cols, cols)
        return pltpu.make_async_copy(
            w_in.at[:, pl.ds(at, cols)], wgt.at[lax.rem(step, 2)], r.w_sem.at[step]
        )

    for copy in loads:
        copy.start()

    barrier = pltpu.get_barrier_semaphore()
    for d in range(1, n_req):
        pl.semaphore_signal(
            barrier, inc=1, device_id={"req": lax.rem(me + d, n_req)}, device_id_type=MESH
        )
    for d in range(1, n_tp):
        pl.semaphore_signal(
            barrier, inc=1, device_id={"tp": lax.rem(tp + d, n_tp)}, device_id_type=MESH
        )
    pl.semaphore_wait(barrier, n_req + n_tp - 2)

    def send(src, dst, ss, rs, to):
        return pltpu.make_async_remote_copy(
            src_ref=src, dst_ref=dst, send_sem=ss, recv_sem=rs,
            device_id={"req": to}, device_id_type=MESH,
        )

    def farx_copy(j):
        return send(r.s_farx.at[j], relay.at[j], r.farx_ss.at[j], r.relay_rs.at[j], mirror)

    def near_copy(k):
        return send(
            r.s_near.at[k - 1], direct.at[me], r.near_ss.at[k - 1], r.direct_rs.at[me], near(k)
        )

    def far_copy(k):
        return send(r.s_far.at[k], direct.at[me], r.far_ss.at[k], r.direct_rs.at[me], far(k))

    def got(ref, rs, o):
        send(ref.at[o], ref.at[o], r.core_ss.at[0], rs.at[o], mirror).wait_recv()

    def nearx_copy(k):
        return send(
            r.s_nearx.at[k - 1], extra.at[me], r.nearx_ss.at[k - 1], r.extra_rs.at[me], near(k)
        )

    def relay_copy(k):
        return send(
            r.s_relay.at[k - 1], extra.at[mirror], r.relay_ss.at[k - 1], r.extra_rs.at[mirror],
            near(k),
        )

    def mate_copy():
        return send(r.s_mate, extra.at[at_near], r.mate_ss, r.mate_rs, mate)

    def pool_copy(k):
        return send(
            r.s_pool.at[k], extra.at[at_pool + k], r.pool_ss.at[k], r.pool_rs.at[k], zmate
        )

    def pass_copy(k):
        return send(
            relay.at[k], extra.at[at_passed + k], r.pass_ss.at[k], r.pass_rs.at[k], mate
        )

    def forward_copy(k):
        return send(
            extra.at[at_pool + k], extra.at[at_forward + k], r.forward_ss.at[k],
            r.forward_rs.at[k], mate,
        )

    for copy in loads:
        copy.wait()
    @pl.loop(0, few)
    def _(j):
        r.s_farx[j] = own[tbl[place["far"] + j]]
        farx_copy(j).start()

    if pool:
        r.s_mate[...] = own[tbl[place["extra"] + mate]]
        mate_copy().start()
        r.s_pool[0] = own[tbl[place["pool"]]]
        pool_copy(0).start()

    def start_near():
        @pl.loop(1, half)
        def _(k):
            r.s_near[k - 1] = own[tbl[place["direct"] + near(k)]]
            near_copy(k).start()
            if not pool:
                r.s_nearx[k - 1] = own[tbl[place["extra"] + near(k)]]
                nearx_copy(k).start()

    def start_far(low, high):
        @pl.loop(low, high)
        def _(k):
            r.s_far[k] = own[tbl[place["direct"] + far(k)]]
            far_copy(k).start()

    early = first if pool else half
    start_near()
    start_far(0, early)

    tok_load.start()
    for step in range(2):
        w_load(step).start()
    direct[me] = own[tbl[place["direct"] + me]]
    extra[at_own if pool else me] = own[tbl[place["extra"] + me]]
    if pool:
        for k in range(1, pool):
            r.s_pool[k] = own[tbl[place["pool"] + k]]

    tok_load.wait()
    tile = 2 if blocks % 2 == 0 else 1

    def product(step, g):
        rows = tok[pl.ds(g * tile, tile)].reshape(tile * BLOCK, feat)
        return jnp.dot(rows, wgt[lax.rem(step, 2)], preferred_element_type=jnp.float32)

    def core_copy(q):
        return pltpu.make_async_remote_copy(
            src_ref=r.cs.at[q], dst_ref=r.cr.at[q], send_sem=r.core_ss.at[q],
            recv_sem=r.core_rs.at[q], device_id={"tp": tp_mate}, device_id_type=MESH,
        )

    def x_copy(q):
        to = 2 * lax.rem(chip + 1 + q, chips) + core
        return pltpu.make_async_remote_copy(
            src_ref=r.cr.at[q], dst_ref=r.xr.at[q], send_sem=r.x_ss.at[q], recv_sem=r.x_rs.at[q],
            device_id={"tp": to}, device_id_type=MESH,
        )

    @pl.loop(0, n_tp)
    def _(step):
        q = lax.rem(step, chips)
        w_load(step).wait()

        @pl.when(step < chips)
        def _():
            @pl.loop(0, blocks // tile)
            def _(g):
                r.cs[q, pl.ds(g * tile, tile)] = (
                    product(step, g).astype(r.cs.dtype).reshape(tile, BLOCK, cols)
                )

            core_copy(q).start()

        @pl.when(step >= chips)
        def _():
            core_copy(q).wait()

            @pl.loop(0, blocks // tile)
            def _(g):
                at = pl.ds(g * tile, tile)
                mine = product(step, g).reshape(tile, BLOCK, cols)
                r.cr[q, at] = (mine + r.cr[q, at].astype(jnp.float32)).astype(r.cr.dtype)

            @pl.when(q < chips - 1)
            def _():
                x_copy(q).start()

        @pl.when(step + 2 < n_tp)
        def _():
            w_load(step + 2).start()

    @pl.loop(0, few)
    def _(j):
        farx_copy(j).wait()

    if pool:

        @pl.loop(0, few)
        def _(j):
            pass_copy(j).start()

        for k in range(1, pool):
            r.s_pool[k] = jnp.where(
                tbl[place["pool_own"] + k] > 0,
                r.s_pool[k],
                relay[tbl[place["pool_relay"] + k]],
            )
            pool_copy(k).start()

        @pl.loop(0, few)
        def _(j):
            extra[at_relay + j] = relay[j]

        start_far(early, half)
        for k in range(pool):
            pool_copy(k).wait_recv()
            forward_copy(k).start()
    else:
        extra[mirror] = relay[tbl[place["pick"] + me]]

        @pl.loop(1, half)
        def _(k):
            r.s_relay[k - 1] = relay[tbl[place["pick"] + near(k)]]
            relay_copy(k).start()

    def part_copy(d, o):
        to = lax.rem(tp + d, n_tp)
        return pltpu.make_async_remote_copy(
            src_ref=r.part.at[to // chips, o], dst_ref=r.landed.at[d - 1, o],
            send_sem=r.part_ss.at[d - 1, o], recv_sem=r.part_rs.at[d - 1, o],
            device_id={"tp": to}, device_id_type=MESH,
        )

    def at_extra(o):
        return tbl[place["at"] + o] if pool else o

    def other(o):
        later = tok[tbl[place["blk1"] + o]]
        return jnp.dot(later, extra[at_extra(o), :feat], preferred_element_type=jnp.float32)

    def shrink(o):
        first = tok[tbl[place["blk0"] + o]]
        later = tok[tbl[place["blk1"] + o]]
        differ = tbl[place["differ"] + o] > 0
        one = jnp.dot(first, direct[o, :feat], preferred_element_type=jnp.float32)
        two = jnp.dot(later, direct[o, :feat], preferred_element_type=jnp.float32)
        alt = r.total[o] if pool else other(o).astype(r.total.dtype)
        two = jnp.where(differ, alt, two.astype(r.part.dtype))
        one = one.astype(r.part.dtype)
        r.part[0, o] = jnp.concatenate([one[:, :rank], two[:, :rank]], axis=1)
        r.part[1, o] = jnp.concatenate([one[:, rank:], two[:, rank:]], axis=1)
        for d in range(1, n_tp):
            part_copy(d, o).start()

    if pool:
        mate_copy().wait_recv()

        @pl.loop(0, few)
        def _(j):
            pass_copy(j).wait()

        for k in range(pool):
            forward_copy(k).wait()

        @pl.loop(0, n_req)
        def _(o):
            r.total[o] = other(o).astype(r.total.dtype)

    def finish(o):
        acc = r.part[tp // chips, o].astype(jnp.float32)
        for d in range(1, n_tp):
            part_copy(d, o).wait()
            acc = acc + r.landed[d - 1, o].astype(jnp.float32)
        acc = acc.astype(r.part.dtype)
        up = direct[o, pl.ds(feat, up_rows)]
        alt = extra[at_extra(o), pl.ds(feat, up_rows)]
        alt = jnp.where(tbl[place["differ"] + o] > 0, alt, up)
        for nth, (mine, maps) in enumerate(((acc[:, :rank], up), (acc[:, rank:], alt))):
            for c in range(cols // LANES):
                r.delta[2 * o + nth, :, c * LANES:(c + 1) * LANES] = jnp.dot(
                    mine, maps[c * rank:(c + 1) * rank], preferred_element_type=jnp.float32
                ).astype(r.delta.dtype)

    def nth_owner(k):
        return jnp.where(k < half, near(k), far(lax.rem(n_req - k, half)))

    @pl.loop(0, n_req + 1)
    def _(k):
        @pl.when(k < n_req)
        def _():
            o = nth_owner(k)

            @pl.when(k > 0)
            def _():
                got(direct, r.direct_rs, o)

            if not pool:

                @pl.when((k > 0) & (o != mirror))
                def _():
                    got(extra, r.extra_rs, o)

            shrink(o)

        @pl.when(k > 0)
        def _():
            finish(nth_owner(k - 1))

    for q in range(chips - 1):
        x_copy(q).wait()

    def store(b):
        return pltpu.make_async_copy(r.cr.at[chips - 1, b], out.at[b], r.out_sem.at[b])

    @pl.loop(0, blocks)
    def _(b):
        delta = r.delta[2 * tbl[place["own"] + b] + tbl[place["second"] + b]]
        delta = jnp.where(tbl[place["live"] + b] > 0, delta.astype(jnp.float32), 0.0)
        acc = r.cr[chips - 1, b].astype(jnp.float32)
        for q in range(chips - 1):
            acc = acc + r.xr[q, b].astype(jnp.float32)
        r.cr[chips - 1, b] = (acc + delta).astype(r.cr.dtype)
        store(b).start()


    @pl.loop(1, half)
    def _(k):
        near_copy(k).wait_send()
        if not pool:
            nearx_copy(k).wait_send()
            relay_copy(k).wait_send()

    @pl.loop(0, half)
    def _(k):
        far_copy(k).wait_send()

    if pool:
        mate_copy().wait_send()
        for k in range(pool):
            pool_copy(k).wait_send()

    @pl.loop(0, blocks)
    def _(b):
        store(b).wait()


def fused(
    tbl, tokens, weight, downs, ups, n_req, n_tp, slots, pool, first, place, ident
):
    rows, feat = tokens.shape
    blocks = rows // BLOCK
    entries, _, width = downs.shape
    rank, cols = ups.shape[1:]
    half, chips, most = n_req // 2, n_tp // 2, max(slots)
    kind = tokens.dtype
    slot = (feat + rank * cols // LANES, width)
    tiles = (blocks, BLOCK, cols)
    vmem = lambda *shape: pltpu.VMEM(shape, kind)
    dma = lambda *shape: pltpu.SemaphoreType.DMA(shape)
    one = pltpu.SemaphoreType.DMA
    scratch = dict(
        own=vmem(entries, *slot),
        tok=vmem(blocks, BLOCK, feat),
        wgt=vmem(2, feat, cols),
        s_near=vmem(half - 1, *slot),
        s_far=vmem(half, *slot),
        s_farx=vmem(most, *slot),
        relay=vmem(most, *slot),
        direct=vmem(n_req, *slot),
        cs=vmem(chips, *tiles),
        cr=vmem(chips, *tiles),
        xr=vmem(chips - 1, *tiles),
        part=vmem(2, n_req, BLOCK, width),
        landed=vmem(n_tp - 1, n_req, BLOCK, width),
        total=vmem(n_req, BLOCK, width),
        delta=vmem(2 * n_req, *tiles[1:]),
        load_sem=dma(2 + cols // LANES),
        w_sem=dma(n_tp),
        near_ss=dma(half - 1),
        far_ss=dma(half),
        direct_rs=dma(n_req),
        farx_ss=dma(most),
        relay_rs=dma(most),
        core_ss=dma(chips),
        core_rs=dma(chips),
        x_ss=dma(chips - 1),
        x_rs=dma(chips - 1),
        part_ss=dma(n_tp - 1, n_req),
        part_rs=dma(n_tp - 1, n_req),
        out_sem=dma(blocks),
    )
    if pool:
        scratch.update(
            extra=vmem(spots(most, pool)[-1], *slot),
            s_mate=vmem(*slot), mate_ss=one, mate_rs=one,
            s_pool=vmem(pool, *slot), pool_ss=dma(pool), pool_rs=dma(pool),
            pass_ss=dma(most), pass_rs=dma(most),
            forward_ss=dma(pool), forward_rs=dma(pool),
        )
    else:
        scratch.update(
            extra=vmem(n_req, *slot), extra_rs=dma(n_req),
            s_nearx=vmem(half - 1, *slot), nearx_ss=dma(half - 1),
            s_relay=vmem(half - 1, *slot), relay_ss=dma(half - 1),
        )
    any_spec = pl.BlockSpec(memory_space=pl.ANY)
    out = pl.pallas_call(
        functools.partial(body, n_req, n_tp, slots, pool, first, place, tuple(scratch)),
        in_specs=[pl.BlockSpec(memory_space=pltpu.SMEM)] + [any_spec] * 4,
        out_specs=any_spec,
        out_shape=jax.ShapeDtypeStruct(tiles, kind),
        scratch_shapes=list(scratch.values()),
        compiler_params=pltpu.CompilerParams(
            collective_id=ident, has_side_effects=True, vmem_limit_bytes=VMEM_BYTES
        ),
        cost_estimate=pl.CostEstimate(
            flops=2 * rows * feat * (n_tp * cols + width),
            bytes_accessed=4 * rows * feat,
            transcendentals=0,
        ),
    )(tbl, tokens.reshape(blocks, BLOCK, feat), weight, downs, ups)
    return out.reshape(rows, cols)


def per_device(tokens, weight, downs, ups, ids, storage):
    n_req, n_tp = lax.axis_size("req"), lax.axis_size("tp")
    half, blocks = n_req // 2, tokens.shape[0] // BLOCK
    plans = PLANS if n_req == 2 * PLANES else []
    table, plan, place = routes(ids, storage, n_req, blocks, downs.shape[0], plans)
    runs = [
        functools.partial(
            fused, n_req=n_req, n_tp=n_tp, slots=(c_in, c_out), pool=pool, first=first,
            place=place, ident=k,
        )
        for k, (c_in, c_out, pool, first) in enumerate(plans + [(half, half, 0, 0)])
    ]
    return lax.switch(plan, runs, table, tokens, weight, downs, ups)


def solution(mesh):
    placed = (P("req", "tp"), P("tp", None), P("req", "tp", None), P("req", None, "tp"), P(), P())
    return jax.shard_map(
        per_device, mesh=mesh, in_specs=placed, out_specs=P("req", "tp"), check_vma=False
    )
```
